128 devices in a mesh: row: 16 (over x, y), col: 8 (over z, core).
Axes of the slice: x: 4, y: 4, z: 4, core: 2. Of those that a mesh axis runs over, the one named last changes fastest.
Arguments:
- trial_vectors: float32 [32768, 256], P(('row', 'col')), may hold values from -6 to 6
- tiles: float32 [16, 8, 128, 128, 128], P('row', 'col'), may hold values from 0.0012207031 to 0.024414062
- tile_rows: int32 [16, 8, 128], P('row', 'col'), may hold values from 0 to 15
- tile_cols: int32 [16, 8, 128], P('row', 'col'), may hold values from 0 to 31
- tile_count: int32 [16, 8], P('row', 'col'), may hold values from 1 to 128, as said below
Outputs:
- basis: float32 [32768, 256], P(('row', 'col'))
The draws below stay inside these ranges and needn't reach their ends.
Inputs may be any that keep to these rules, and one draw needn't show every extreme that they name: `tile_count`: slots at or beyond a device's count are not part of the graph; some slab and column group holds exactly 128 live slots.
All inputs are finite; a program needn't handle non-finite values.
Results may differ from the reference program's by a relative error of at most 0.0003.
Values sent between devices are 32-bit elements; how exact they have to be, the bound alone decides.
No kernel may reach another device: no remote copies, remote signals or barrier semaphores. Data moves between devices by JAX's collectives and lax.ppermute only.
A program may use at most 128 MiB of HBM per device.

```python
import math
import jax
import jax.numpy as jnp
from jax import lax

BLK = 128
K = 256
NBD = 2
CAP = 128
ITERS = 2
SLAB_B = 16
MEMBERS = 32
NODES = 32768
N_ROW = 16
N_COL = 8


def draw_tile_count(key, part):
    first_key, second_key = jax.random.split(key)
    divisor = 1 + jax.random.randint(first_key, (N_ROW, N_COL), 0, 5)
    counts = (CAP // divisor).reshape(-1)
    fullest = jax.random.randint(second_key, (), 0, N_ROW * N_COL)
    counts = jnp.where(jnp.arange(N_ROW * N_COL) == fullest, CAP, counts)
    return counts.reshape(N_ROW, N_COL).astype(jnp.int32)


def place_ends(entries, key, least, largest):
    place = [jax.random.randint(jax.random.fold_in(key, axis), (), 0, length) for axis, length in enumerate(entries.shape)]
    widest = entries.shape.index(max(entries.shape))
    beside = place[:widest] + [(place[widest] + 1) % entries.shape[widest]] + place[widest + 1:]
    return entries.at[tuple(place)].set(least).at[tuple(beside)].set(largest)


def shard_levels(own_key, extent, shards, low, top_value):
    level, own = 1.0, jax.random.fold_in(own_key, 6)
    for position, parts in shards:
        heights = jnp.exp(jax.random.uniform(jax.random.fold_in(own, position), (parts,), jnp.float32, low / len(shards), top_value / len(shards)))
        level = level * jnp.repeat(heights, extent[position] // parts).reshape([-1 if axis == position else 1 for axis in range(len(extent))])
    return level


def scatter_about(stream_key, extent, spread, bound, cuts=(), held_as=jnp.bfloat16):
    loudness = shard_levels(stream_key, extent, cuts, -0.22, 0.18) if cuts else 1.0
    values = jax.random.normal(stream_key, extent, jnp.float32) * spread * loudness
    return jnp.minimum(jnp.maximum(values, -bound), bound).astype(held_as)


def setup_inputs(seed: int = 0) -> dict:
    streams_of = jax.random.split(jax.random.key(seed), 6)
    return {
        "trial_vectors": scatter_about(streams_of[0], (NODES, K), 1.0, 6.0, ((0, 128),), jnp.float32),
        "tiles": jnp.clip(jnp.exp(math.log(0.024414062) - 2.9957323 * jax.random.uniform(streams_of[1], (N_ROW, N_COL, CAP, BLK, BLK), jnp.float32) ** shard_levels(streams_of[1], (N_ROW, N_COL, CAP, BLK, BLK), ((0, 16), (1, 8)), -0.2, 0.2)), 0.0012207031, 0.024414062),
        "tile_rows": place_ends(jax.random.randint(streams_of[2], (N_ROW, N_COL, CAP), 0, SLAB_B), jax.random.fold_in(streams_of[2], 1), 0, SLAB_B - 1).astype(jnp.int32),
        "tile_cols": place_ends(jax.random.randint(streams_of[3], (N_ROW, N_COL, CAP), 0, MEMBERS), jax.random.fold_in(streams_of[3], 1), 0, MEMBERS - 1).astype(jnp.int32),
        "tile_count": draw_tile_count(jax.random.fold_in(streams_of[5], 71), 0),
    }


HIGHEST = lax.Precision.HIGHEST

def block_apply(tiles_flat, put_index, take_index, counts, source, out_blocks, adjoint):
    slot_total = tiles_flat.shape[1]
    slot_step = min(32, slot_total)
    size_block = tiles_flat.shape[-1]
    vector_width = source.shape[-1]

    def one_device(running, device_item):
        tiles_dev, put_dev, take_dev, count_dev = device_item

        def one_block(block_number, inner):
            first_slot = block_number * slot_step
            tiles_now = lax.dynamic_slice_in_dim(tiles_dev, first_slot, slot_step, 0)
            put_now = lax.dynamic_slice_in_dim(put_dev, first_slot, slot_step, 0)
            take_now = lax.dynamic_slice_in_dim(take_dev, first_slot, slot_step, 0)
            alive_mask = first_slot + jnp.arange(slot_step) < count_dev
            picked = source[take_now]
            if adjoint:
                product = jnp.einsum('sij,sik->sjk', tiles_now, picked, precision=HIGHEST)
            else:
                product = jnp.einsum('sij,sjk->sik', tiles_now, picked, precision=HIGHEST)
            product = jnp.where(alive_mask[:, None, None], product, jnp.zeros_like(product))
            return inner.at[put_now].add(product)
        upper_bound = ((count_dev + slot_step - 1) // slot_step).astype(jnp.int32)
        return (lax.fori_loop(jnp.int32(0), upper_bound, one_block, running), None)
    initial = jnp.zeros((out_blocks, size_block, vector_width), jnp.float32)
    result, unused = lax.scan(one_device, initial, (tiles_flat, put_index, take_index, counts))
    return result

def reference(trial_vectors, tiles, tile_rows, tile_cols, tile_count):
    devices_all = N_ROW * N_COL
    blocks_all = NODES // BLK
    tiles_flat = tiles.reshape(devices_all, CAP, BLK, BLK)
    row_axis = (jnp.arange(devices_all) // N_COL).astype(jnp.int32)
    col_axis = (jnp.arange(devices_all) % N_COL).astype(jnp.int32)
    rows_global = (row_axis[:, None] * SLAB_B + tile_rows.reshape(devices_all, CAP)).astype(jnp.int32)
    members = tile_cols.reshape(devices_all, CAP)
    cols_global = (members // NBD * SLAB_B + col_axis[:, None] * NBD + members % NBD).astype(jnp.int32)
    counts = tile_count.reshape(devices_all).astype(jnp.int32)
    all_ones = jnp.ones((blocks_all, BLK, 1), jnp.float32)
    row_sums = block_apply(tiles_flat, rows_global, cols_global, counts, all_ones, blocks_all, False)[..., 0]
    inverse = 1.0 / (1.0 + row_sums)
    tilde_part = block_apply(tiles_flat, rows_global, cols_global, counts, inverse[..., None], blocks_all, False)[..., 0]
    tilde_degree = inverse * (inverse + tilde_part)
    row_scale = inverse / tilde_degree
    vectors = trial_vectors.reshape(blocks_all, BLK, K)
    for iteration in range(ITERS):
        scaled = inverse[..., None] * vectors
        forward = block_apply(tiles_flat, rows_global, cols_global, counts, scaled, blocks_all, False) + scaled
        weighted = row_scale[..., None] * (row_scale[..., None] * forward)
        backward = block_apply(tiles_flat, cols_global, rows_global, counts, weighted, blocks_all, True) + weighted
        node_rows = (inverse[..., None] * backward).reshape(NODES, K)
        gram_matrix = jnp.dot(node_rows.T.astype(jnp.float32), node_rows.astype(jnp.float32), precision=HIGHEST, preferred_element_type=jnp.float32)
        factor_low = jnp.linalg.cholesky(gram_matrix)
        solved = lax.linalg.triangular_solve(factor_low, node_rows, left_side=False, lower=True, transpose_a=True)
        vectors = solved.reshape(blocks_all, BLK, K)
    return vectors.reshape(NODES, K) * jnp.sqrt(jnp.float32(NODES))
```

```python
import functools
import math

import jax
import jax.numpy as jnp
from jax import lax
from jax.experimental import pallas as pl
from jax.experimental.pallas import tpu as pltpu
from jax.sharding import Mesh
from jax.sharding import PartitionSpec as P

ITERS = 2
HIGHEST = lax.Precision.HIGHEST
F32 = jnp.float32
BF16 = jnp.bfloat16
BLK = 128
CHUNK = 16
RING = range(4)


def shift(value, axis, amount):
    return lax.ppermute(value, axis, [(i, (i + amount) % 4) for i in RING])


def swap(value):
    return lax.ppermute(value, "c", [(0, 1), (1, 0)])


def ring_all(value, axis):
    return [value] + [shift(value, axis, k) for k in (1, 2, 3)]


def ring_sum(value, axis):
    a, b, c, d = ring_all(value, axis)
    return (a + b) + (c + d)


def ring_scatter(pieces, axis):
    a = pieces[0]
    b, c, d = [shift(pieces[k], axis, k) for k in (1, 2, 3)]
    return (a + b) + (c + d)


def split(value):
    high = value.astype(BF16)
    return high, (value - high.astype(F32)).astype(BF16)


def nt_dot(a, b, precision=HIGHEST):
    return lax.dot_general(
        a, b, (((1,), (1,)), ((), ())), precision=precision, preferred_element_type=F32
    )


def lane_sums(block):
    return nt_dot(jnp.ones((8, block.shape[1]), F32), block)[0:1, :]


def live_tile(tiles_ref, slot, first, count):
    return jnp.where(first + slot < count, tiles_ref[slot], 0.0)


def rowsum_kernel(count_ref, put_ref, tiles_ref, out_ref, total):
    step = pl.program_id(0)
    count = count_ref[0]

    @pl.when(step == 0)
    def _():
        total[...] = jnp.zeros_like(total)

    first = step * CHUNK

    @pl.when(first < count)
    def _():
        def one(slot, carry):
            block = put_ref[first + slot]
            total[block] += live_tile(tiles_ref, slot, first, count)
            return carry

        lax.fori_loop(0, CHUNK, one, 0)

    @pl.when(step == pl.num_programs(0) - 1)
    def _():
        for block in range(total.shape[0]):
            out_ref[block : block + 1, :] = lane_sums(total[block])


def chunk_map(step, count_ref, *_):
    return (jnp.minimum(step, (count_ref[0] + CHUNK - 1) // CHUNK - 1), 0, 0)


def rowsum_call(count, put, tiles, out_blocks):
    slots = tiles.shape[0]
    return pl.pallas_call(
        rowsum_kernel,
        out_shape=jax.ShapeDtypeStruct((out_blocks, BLK), F32),
        grid_spec=pltpu.PrefetchScalarGridSpec(
            num_scalar_prefetch=2,
            grid=(slots // CHUNK,),
            in_specs=[pl.BlockSpec((CHUNK, BLK, BLK), chunk_map)],
            out_specs=pl.BlockSpec((out_blocks, BLK), lambda s, *_: (0, 0)),
            scratch_shapes=[pltpu.VMEM((out_blocks, BLK, BLK), F32)],
        ),
        cost_estimate=pl.CostEstimate(flops=10**6, bytes_accessed=2**23, transcendentals=0),
    )(count, put, tiles)


def apply_loop(
    count, first, put_ref, take_ref, tiles_ref, source, total, adjoint, tilde, inverse_ref
):
    def one(slot, carry):
        tile = live_tile(tiles_ref, slot, first, count)
        take = take_ref[first + slot]
        put = pl.multiple_of(put_ref[first + slot], 8)
        if tilde is not None:
            tilde_block = carry_block = put_ref[tiles_total(put_ref) + first + slot]
            tilde[tilde_block] += tile * inverse_ref[pl.ds(take, 1), :]
        if adjoint:
            tile = tile.T
        high, low = split(tile)
        product = jnp.dot(
            jnp.concatenate([high, high], axis=1), source[take], preferred_element_type=F32
        ) + jnp.dot(low, source[take, :BLK], preferred_element_type=F32)
        total[pl.ds(put, BLK), :] += product
        return carry

    lax.fori_loop(0, CHUNK, one, 0, unroll=4)


def tiles_total(put_ref):
    return put_ref.shape[0] // 2


def put_source(source, index, value):
    high, low = split(value)
    source[index, :BLK] = high
    source[index, BLK:] = low


def forward_kernel(first_pass, *refs):
    count_ref, put_ref, take_ref, tiles_ref, inverse_ref = refs[:5]
    factor_ref = None
    refs = refs[5:]
    if not first_pass:
        factor_ref, refs = refs[0], refs[1:]
    pieces, (keep_ref, send_ref), refs = refs[:8], refs[8:10], refs[10:]
    source, total = refs[:2]
    tilde = refs[2] if first_pass else None
    step = pl.program_id(0)
    count = count_ref[0]
    first = step * CHUNK

    @pl.when(step == 0)
    def _():
        total[...] = jnp.zeros_like(total)
        if first_pass:
            tilde[...] = jnp.zeros_like(tilde)
        inverse = inverse_ref[...].T
        for number, piece in enumerate(pieces):
            if first_pass:
                values = None
            else:
                values = nt_dot(piece[...].reshape(4 * BLK, -1), factor_ref[...])
            for part in RING:
                index = number * 4 + part
                value = piece[part] if first_pass else values[part * BLK : (part + 1) * BLK]
                put_source(source, index, value * inverse[:, index : index + 1])

    @pl.when(first < count)
    def _():
        apply_loop(
            count, first, put_ref, take_ref, tiles_ref, source, total, False, tilde, inverse_ref
        )

    @pl.when(step == pl.num_programs(0) - 1)
    def _():
        rows = keep_ref.shape[1]
        for number in range(8):
            if first_pass:
                line = jnp.concatenate(
                    [lane_sums(tilde[2 * number]), lane_sums(tilde[2 * number + 1])], axis=1
                )
                total[number * rows + 2 * BLK : (number + 1) * rows, :] = jnp.broadcast_to(
                    line, (rows - 2 * BLK, line.shape[1])
                )
            target = keep_ref if number < 4 else send_ref
            target[number % 4] = total[number * rows : (number + 1) * rows, :]


def whole(shape):
    return pl.BlockSpec(shape, lambda s, *_: (0,) * len(shape), pipeline_mode=pl.Buffered(1))


def forward_call(count, put, take, tiles, inverse, factor, pieces):
    first_pass = factor is None
    slots = tiles.shape[0]
    width = pieces[0].shape[-1]
    rows = 2 * BLK + (8 if first_pass else 0)
    extra = [] if first_pass else [factor]
    out = jax.ShapeDtypeStruct((4, rows, width), F32)
    scratch = [pltpu.VMEM((32, 2 * BLK, width), BF16), pltpu.VMEM((8 * rows, width), F32)]
    if first_pass:
        scratch.append(pltpu.VMEM((16, BLK, BLK), F32))
    return pl.pallas_call(
        functools.partial(forward_kernel, first_pass),
        out_shape=(out, out),
        grid_spec=pltpu.PrefetchScalarGridSpec(
            num_scalar_prefetch=3,
            grid=(slots // CHUNK,),
            in_specs=[pl.BlockSpec((CHUNK, BLK, BLK), chunk_map)]
            + [whole(a.shape) for a in [inverse] + extra + list(pieces)],
            out_specs=(whole(out.shape), whole(out.shape)),
            scratch_shapes=scratch,
        ),
        cost_estimate=pl.CostEstimate(
            flops=6 * 2**30, bytes_accessed=2**24, transcendentals=0
        ),
    )(count, put, take, tiles, inverse, *extra, *pieces)


def backward_kernel(*refs):
    count_ref, put_ref, take_ref, tiles_ref = refs[:4]
    pieces, outs, (source, total) = refs[4:12], refs[12:20], refs[20:]
    step = pl.program_id(0)
    count = count_ref[0]
    first = step * CHUNK

    @pl.when(step == 0)
    def _():
        total[...] = jnp.zeros_like(total)
        for number, piece in enumerate(pieces):
            for part in range(2):
                put_source(source, number * 2 + part, piece[part * BLK : (part + 1) * BLK])

    @pl.when(first < count)
    def _():
        apply_loop(count, first, put_ref, take_ref, tiles_ref, source, total, True, None, None)

    @pl.when(step == pl.num_programs(0) - 1)
    def _():
        for number, out in enumerate(outs):
            for part in RING:
                start = (number * 4 + part) * BLK
                out[part] = total[start : start + BLK, :]


def backward_call(count, put, take, tiles, pieces):
    slots = tiles.shape[0]
    width = pieces[0].shape[-1]
    out = jax.ShapeDtypeStruct((4, BLK, width), F32)
    return pl.pallas_call(
        backward_kernel,
        out_shape=(out,) * 8,
        grid_spec=pltpu.PrefetchScalarGridSpec(
            num_scalar_prefetch=3,
            grid=(slots // CHUNK,),
            in_specs=[pl.BlockSpec((CHUNK, BLK, BLK), chunk_map)]
            + [whole(a.shape) for a in pieces],
            out_specs=(whole(out.shape),) * 8,
            scratch_shapes=[
                pltpu.VMEM((16, 2 * BLK, width), BF16),
                pltpu.VMEM((32 * BLK, width), F32),
            ],
        ),
        cost_estimate=pl.CostEstimate(
            flops=6 * 2**30, bytes_accessed=2**24, transcendentals=0
        ),
    )(count, put, take, tiles, *pieces)


PANEL = 32


def inverse_factor_kernel(gram_ref, out_ref, work):
    size = gram_ref.shape[0]
    work[:, :size] = gram_ref[...]
    row_at = lax.broadcasted_iota(jnp.int32, (size, size), 0)
    lane_at = lax.broadcasted_iota(jnp.int32, (size, size), 1)
    work[:, size:] = (row_at == lane_at).astype(F32)
    rows = lax.broadcasted_iota(jnp.int32, (PANEL, 1), 0)
    rows_small = lax.broadcasted_iota(jnp.int32, (PANEL, PANEL), 0)
    lanes_small = lax.broadcasted_iota(jnp.int32, (PANEL, PANEL), 1)
    unit = (rows_small == lanes_small).astype(F32)
    for start in range(0, size, PANEL):
        end = start + PANEL
        pair = jnp.concatenate([work[start:end, start:end], unit], axis=1)
        for j in range(PANEL - 1):
            row = pair[j : j + 1, :] / pair[j : j + 1, j : j + 1]
            pair = pair - jnp.where(rows > j, pair[:, j : j + 1], 0.0) * row
        pivots = jnp.sum(pair[:, :PANEL] * unit, axis=1, keepdims=True)
        corner = pair[:, PANEL:] * (1.0 / jnp.sqrt(pivots))
        panel = jnp.dot(corner, work[start:end, :], precision=HIGHEST, preferred_element_type=F32)
        work[start:end, :] = panel
        if end < size:
            update = lax.dot_general(
                panel[:, :size],
                panel,
                (((0,), (0,)), ((), ())),
                precision=HIGHEST,
                preferred_element_type=F32,
            )
            work[end:, :] -= update[end:, :]
    out_ref[...] = work[:, size:]


def inverse_factor(gram):
    size = gram.shape[0]
    return pl.pallas_call(
        inverse_factor_kernel,
        out_shape=jax.ShapeDtypeStruct((size, size), F32),
        in_specs=[pl.BlockSpec(memory_space=pltpu.VMEM)],
        out_specs=pl.BlockSpec(memory_space=pltpu.VMEM),
        scratch_shapes=[pltpu.VMEM((size, 2 * size), F32)],
        cost_estimate=pl.CostEstimate(flops=2**34, bytes_accessed=2**19, transcendentals=0),
    )(gram)


def gather_row(first, second):
    first = jnp.stack(ring_all(first, "x"))
    second = jnp.stack(ring_all(second, "y"))
    return ring_all(first, "y") + ring_all(second, "x")


def scatter_row(outs):
    first, second = outs[:4], outs[4:]
    first_in = [first[0]] + [shift(first[k], "x", k) for k in (1, 2, 3)]
    second_in = [second[0]] + [shift(second[k], "y", k) for k in (1, 2, 3)]

    def add(parts, i):
        return (parts[0][i] + parts[1][i]) + (parts[2][i] + parts[3][i])

    one = ring_scatter([add(first_in, i) for i in RING], "y")
    two = ring_scatter([add(second_in, i) for i in RING], "x")
    return jnp.concatenate([one, two], axis=0)


def gram_sum(gram):
    half = gram.shape[0] // 2
    core = lax.axis_index("c")
    kept = lax.dynamic_slice_in_dim(gram, core * half, half, 0)
    sent = lax.dynamic_slice_in_dim(gram, (1 - core) * half, half, 0)
    value = kept + swap(sent)
    for axis in "xyz":
        value = ring_sum(value, axis)
    other = swap(value)
    return jnp.where(
        core == 0, jnp.concatenate([value, other]), jnp.concatenate([other, value])
    )


def local(trial_vectors, tiles, tile_rows, tile_cols, tile_count):
    x, y, z, core = [lax.axis_index(a) for a in ("x", "y", "z", "c")]
    slots = tiles.shape[2]
    width = trial_vectors.shape[1]
    tiles = tiles.reshape(slots, BLK, BLK)
    count = tile_count.reshape(1)

    row = tile_rows.reshape(slots)
    col = tile_cols.reshape(slots)
    row_other = ((row // 2) % 2) ^ core
    row_z, row_part = row // 4, row % 2
    put_forward = (row_other * 4 + (row_z - z) % 4) * 2 + row_part
    take_backward = (row_other * 4 + (z - row_z) % 4) * 2 + row_part
    col_x, col_y, col_part = col // 8, (col // 2) % 4, col % 2
    back_x, back_y = (x - col_x) % 4, (y - col_y) % 4
    take_forward = jnp.where(col_part == 0, back_y * 4 + back_x, 16 + back_x * 4 + back_y)
    to_x, to_y = (col_x - x) % 4, (col_y - y) % 4
    put_backward = BLK * jnp.where(col_part == 0, to_x * 4 + to_y, 16 + to_y * 4 + to_x)
    put_first = jnp.concatenate(
        [(put_forward // 2) * (2 * BLK + 8) + (put_forward % 2) * BLK, put_forward]
    )
    put_later = put_forward * BLK

    pieces = gather_row(trial_vectors[:BLK], trial_vectors[BLK:])

    sums = rowsum_call(count, put_forward, tiles, 16)
    sums = (sums[:8] + swap(sums[8:])).reshape(4, 2, BLK)
    inverse_own = 1.0 / (1.0 + ring_scatter(list(sums), "z"))
    gathered = jnp.stack(ring_all(jnp.stack(ring_all(inverse_own, "x")), "y"))
    inverse = jnp.concatenate(
        [gathered[:, :, 0].reshape(16, BLK), gathered[:, :, 1].swapaxes(0, 1).reshape(16, BLK)]
    )
    inverse_own = inverse_own.reshape(2 * BLK, 1)

    vectors = trial_vectors
    factor = None
    scale = None
    for iteration in range(ITERS):
        keep, send = forward_call(
            count,
            put_first if iteration == 0 else put_later,
            take_forward,
            tiles,
            inverse,
            factor,
            pieces,
        )
        summed = ring_scatter(list(keep + swap(send)), "z")
        if iteration == 0:
            tilde = inverse_own * (inverse_own + summed[2 * BLK].reshape(2 * BLK, 1))
            scale = inverse_own / tilde
            summed = summed[: 2 * BLK]
        weighted = scale * (scale * (summed + inverse_own * vectors))
        mine = ring_all(weighted, "z")
        outs = backward_call(
            count, put_backward, take_backward, tiles, mine + [swap(v) for v in mine]
        )
        reduced = inverse_own * (scatter_row(outs) + weighted)
        gram = lax.dot_general(
            reduced,
            reduced,
            (((0,), (0,)), ((), ())),
            precision=HIGHEST,
            preferred_element_type=F32,
        )
        if iteration + 1 < ITERS:
            pieces = gather_row(reduced[:BLK], reduced[BLK:])
        factor = inverse_factor(gram_sum(gram))
        vectors = nt_dot(reduced, factor)
    total_nodes = 2 * BLK * 128
    return vectors * math.sqrt(total_nodes)


def solution(mesh):
    fine = Mesh(mesh.devices.reshape(4, 4, 4, 2), ("x", "y", "z", "c"))
    row, column = ("x", "y"), ("z", "c")
    in_specs = (
        P(row + column, None),
        P(row, column, None, None, None),
        P(row, column, None),
        P(row, column, None),
        P(row, column),
    )
    return jax.shard_map(
        local, mesh=fine, in_specs=in_specs, out_specs=P(row + column, None), check_vma=False
    )
```

```python
import functools
import math

import jax
import jax.numpy as jnp
from jax import lax
from jax.experimental import pallas as pl
from jax.experimental.pallas import tpu as pltpu
from jax.sharding import Mesh
from jax.sharding import PartitionSpec as P

ITERS = 2
HIGHEST = lax.Precision.HIGHEST
F32 = jnp.float32
BF16 = jnp.bfloat16
BLK = 128
HALF = 64
CHUNK = 32
UNROLL = 8


def flip(value, step):
    axis, mask = step
    return lax.ppermute(value, axis, [(i, i ^ mask) for i in range(2 if axis == "c" else 4)])


def gather(value, steps):
    for step in steps[:-1]:
        value = jnp.concatenate([value, flip(value, step)])
    return [value, flip(value, steps[-1])]


def scatter(keep, send, steps):
    for step in reversed(steps[1:]):
        got = flip(send, step)
        half = keep.shape[0] // 2
        keep, send = keep[:half] + got[:half], keep[half:] + got[half:]
    return keep + flip(send, steps[0])


X1, X3, Y1, Y3, Z1, Z3 = [(axis, mask) for axis in "xyz" for mask in (1, 3)]
CORE = ("c", 1)
ROW_STEPS = [[X1, X3, Y1, Y3], [X3, X1, Y3, Y1], [Y1, Y3, X1, X3], [Y3, Y1, X3, X1]]
COL_STEPS = [[Z1, Z3], [Z3, Z1]]


def shift(value, axis, amount):
    return lax.ppermute(value, axis, [(i, (i + amount) % 4) for i in range(4)])


def ring_sum(value, axis):
    return (value + shift(value, axis, 1)) + (shift(value, axis, 2) + shift(value, axis, 3))


def flip_bits(mine, other):
    offset = mine ^ other
    return jnp.where((offset == 1) | (offset == 2), 1, 0), jnp.where(offset >= 2, 1, 0)


def swapped(index):
    return (index & 5) * 2 + (index & 10) // 2


def split(value):
    high = value.astype(BF16)
    return high, (value - high.astype(F32)).astype(BF16)


def nt_dot(a, b, precision=HIGHEST):
    return lax.dot_general(
        a, b, (((1,), (1,)), ((), ())), precision=precision, preferred_element_type=F32
    )


def lane_sums(block):
    return nt_dot(jnp.ones((8, block.shape[1]), F32), block)[0:1, :]


def live_tile(tiles_ref, slot, first, count):
    return jnp.where(first + slot < count, tiles_ref[slot], 0.0)


def rowsum_kernel(count_ref, put_ref, tiles_ref, *refs):
    out_ref, total = refs[-2:]
    step = pl.program_id(0)
    count = count_ref[0]

    @pl.when(step == 0)
    def _():
        total[...] = jnp.zeros_like(total)

    first = step * CHUNK

    @pl.when(first < count)
    def _():
        def one(slot, carry):
            block = put_ref[first + slot]
            total[block] += live_tile(tiles_ref, slot, first, count)
            return carry

        lax.fori_loop(0, CHUNK, one, 0, unroll=UNROLL)

    @pl.when(step == pl.num_programs(0) - 1)
    def _():
        for block in range(total.shape[0]):
            out_ref[block : block + 1, :] = lane_sums(total[block])


def chunk_map(step, count_ref, *_):
    return (jnp.minimum(step, (count_ref[0] + CHUNK - 1) // CHUNK - 1), 0, 0)


def rowsum_call(count, put, tiles, out_blocks, after):
    slots = tiles.shape[0]
    return pl.pallas_call(
        rowsum_kernel,
        out_shape=jax.ShapeDtypeStruct((out_blocks, BLK), F32),
        grid_spec=pltpu.PrefetchScalarGridSpec(
            num_scalar_prefetch=2,
            grid=(slots // CHUNK,),
            in_specs=[pl.BlockSpec((CHUNK, BLK, BLK), chunk_map)]
            + [pl.BlockSpec(memory_space=pl.ANY)] * len(after),
            out_specs=pl.BlockSpec((out_blocks, BLK), lambda s, *_: (0, 0)),
            scratch_shapes=[pltpu.VMEM((out_blocks, BLK, BLK), F32)],
        ),
        cost_estimate=pl.CostEstimate(flops=10**10, bytes_accessed=2**23, transcendentals=0),
    )(count, put, tiles, *after)


def apply_loop(
    count, first, put_ref, take_ref, tiles_ref, source, total, adjoint, tilde, inverse_ref
):
    def one(slot, carry):
        tile = live_tile(tiles_ref, slot, first, count)
        take = take_ref[first + slot]
        put = pl.multiple_of(put_ref[first + slot], 8)
        if tilde is not None:
            tilde_block = put_ref[put_ref.shape[0] // 2 + first + slot]
            tilde[tilde_block] += tile * inverse_ref[pl.ds(take, 1), :]
        if adjoint:
            tile = tile.T
        high, low = split(tile)
        product = jnp.dot(
            jnp.concatenate([high, high], axis=1), source[take], preferred_element_type=F32
        ) + jnp.dot(low, source[take, :BLK], preferred_element_type=F32)
        total[pl.ds(put, BLK), :] += product
        return carry

    lax.fori_loop(0, CHUNK, one, 0, unroll=UNROLL)


def put_source(source, index, row, value):
    high, low = split(value)
    rows = value.shape[0]
    source[index, row : row + rows] = high
    source[index, BLK + row : BLK + row + rows] = low


def piece_place(quarter, index):
    place = index if quarter % 2 == 0 else swapped(index)
    return (quarter // 2) * 16 + place, (quarter % 2) * HALF


def forward_kernel(first_pass, *refs):
    count_ref, put_ref, take_ref, tiles_ref, inverse_ref = refs[:5]
    factor_ref = None
    refs = refs[5:]
    if not first_pass:
        factor_ref, refs = refs[0], refs[1:]
    pieces, (keep_ref, send_ref), refs = refs[:8], refs[8:10], refs[10:]
    source, total = refs[:2]
    tilde = refs[2] if first_pass else None
    step = pl.program_id(0)
    count = count_ref[0]
    first = step * CHUNK

    @pl.when(step == 0)
    def _():
        total[...] = jnp.zeros_like(total)
        if first_pass:
            tilde[...] = jnp.zeros_like(tilde)
        inverse = inverse_ref[...].T
        for number, piece in enumerate(pieces):
            quarter, half = number // 2, number % 2
            if not first_pass:
                values = nt_dot(piece[...].reshape(8 * HALF, -1), factor_ref[...])
            for part in range(8):
                index, row = piece_place(quarter, half * 8 + part)
                value = piece[part] if first_pass else values[part * HALF : (part + 1) * HALF]
                put_source(source, index, row, value * inverse[row : row + HALF, index : index + 1])

    @pl.when(first < count)
    def _():
        apply_loop(
            count, first, put_ref, take_ref, tiles_ref, source, total, False, tilde, inverse_ref
        )

    @pl.when(step == pl.num_programs(0) - 1)
    def _():
        rows = keep_ref.shape[1]
        for number in range(16):
            if first_pass:
                line = lane_sums(tilde[number])
                total[number * rows + BLK : (number + 1) * rows, :BLK] = jnp.broadcast_to(
                    line, (rows - BLK, BLK)
                )
            target = keep_ref if number < 8 else send_ref
            target[number % 8] = total[number * rows : (number + 1) * rows, :]


def whole(shape):
    return pl.BlockSpec(shape, lambda s, *_: (0,) * len(shape), pipeline_mode=pl.Buffered(1))


def forward_call(count, put, take, tiles, inverse, factor, pieces):
    first_pass = factor is None
    slots = tiles.shape[0]
    width = pieces[0].shape[-1]
    rows = BLK + (8 if first_pass else 0)
    extra = [] if first_pass else [factor]
    out = jax.ShapeDtypeStruct((8, rows, width), F32)
    scratch = [pltpu.VMEM((32, 2 * BLK, width), BF16), pltpu.VMEM((16 * rows, width), F32)]
    if first_pass:
        scratch.append(pltpu.VMEM((16, BLK, BLK), F32))
    return pl.pallas_call(
        functools.partial(forward_kernel, first_pass),
        out_shape=(out, out),
        grid_spec=pltpu.PrefetchScalarGridSpec(
            num_scalar_prefetch=3,
            grid=(slots // CHUNK,),
            in_specs=[pl.BlockSpec((CHUNK, BLK, BLK), chunk_map)]
            + [whole(a.shape) for a in [inverse] + extra + list(pieces)],
            out_specs=(whole(out.shape), whole(out.shape)),
            scratch_shapes=scratch,
        ),
        cost_estimate=pl.CostEstimate(
            flops=6 * 2**30, bytes_accessed=2**24, transcendentals=0
        ),
    )(count, put, take, tiles, inverse, *extra, *pieces)


def backward_kernel(*refs):
    count_ref, put_ref, take_ref, tiles_ref = refs[:4]
    pieces, outs, (source, total) = refs[4:12], refs[12:20], refs[20:]
    step = pl.program_id(0)
    count = count_ref[0]
    first = step * CHUNK

    @pl.when(step == 0)
    def _():
        total[...] = jnp.zeros_like(total)
        for number, piece in enumerate(pieces):
            for part in range(2):
                put_source(source, number * 2 + part, 0, piece[part])

    @pl.when(first < count)
    def _():
        apply_loop(count, first, put_ref, take_ref, tiles_ref, source, total, True, None, None)

    @pl.when(step == pl.num_programs(0) - 1)
    def _():
        for number, out in enumerate(outs):
            for part in range(8):
                index, row = piece_place(number // 2, number % 2 * 8 + part)
                out[part] = total[index * BLK + row : index * BLK + row + HALF, :]


def backward_call(count, put, take, tiles, pieces):
    slots = tiles.shape[0]
    width = pieces[0].shape[-1]
    out = jax.ShapeDtypeStruct((8, HALF, width), F32)
    return pl.pallas_call(
        backward_kernel,
        out_shape=(out,) * 8,
        grid_spec=pltpu.PrefetchScalarGridSpec(
            num_scalar_prefetch=3,
            grid=(slots // CHUNK,),
            in_specs=[pl.BlockSpec((CHUNK, BLK, BLK), chunk_map)]
            + [whole(a.shape) for a in pieces],
            out_specs=(whole(out.shape),) * 8,
            scratch_shapes=[
                pltpu.VMEM((16, 2 * BLK, width), BF16),
                pltpu.VMEM((32 * BLK, width), F32),
            ],
        ),
        cost_estimate=pl.CostEstimate(
            flops=6 * 2**30, bytes_accessed=2**24, transcendentals=0
        ),
    )(count, put, take, tiles, *pieces)


PANEL = 32


def inverse_factor_kernel(gram_ref, out_ref, work, columns, multiplier, right):
    size = gram_ref.shape[0]
    lanes = columns.shape[-1]
    work[:, :size] = gram_ref[...]
    row_at = lax.broadcasted_iota(jnp.int32, (size, size), 0)
    lane_at = lax.broadcasted_iota(jnp.int32, (size, size), 1)
    work[:, size:] = (row_at == lane_at).astype(F32)
    row_small = lax.broadcasted_iota(jnp.int32, (PANEL, lanes), 0)
    lane_small = lax.broadcasted_iota(jnp.int32, (PANEL, lanes), 1)
    unit = (row_small == lane_small).astype(F32)
    for start in range(0, size, PANEL):
        end = start + PANEL
        corner = work[start:end, start:end]
        for k in range(PANEL):
            columns[k] = jnp.broadcast_to(corner[:, k : k + 1], (PANEL, lanes))
        right[...] = unit
        for j in range(PANEL - 1):
            low = 8 * ((j + 1) // 8)
            column = columns[j, low:, :]
            factor = jnp.where(row_small[low:] > j, column, 0.0) * (1.0 / columns[j, j : j + 1, :])
            multiplier[low:, :] = factor
            for k in range(j + 1, PANEL):
                k_low = 8 * (k // 8)
                columns[k, k_low:, :] -= column[k_low - low :] * multiplier[k : k + 1, :]
            right[low:, :] -= factor * right[j : j + 1, :]
        pivots = jnp.concatenate([columns[k, k : k + 1, :] for k in range(PANEL)], axis=0)
        corner = (right[...] * (1.0 / jnp.sqrt(pivots)))[:, :PANEL]
        left = lanes * (start // lanes)
        used = size + lanes * ((end + lanes - 1) // lanes)
        panel = jnp.dot(
            corner, work[start:end, left:used], precision=HIGHEST, preferred_element_type=F32
        )
        work[start:end, left:used] = panel
        if end < size:
            update = lax.dot_general(
                panel[:, : size - left],
                panel,
                (((0,), (0,)), ((), ())),
                precision=HIGHEST,
                preferred_element_type=F32,
            )
            work[end:, left:used] -= update[end - left :, :]
    out_ref[...] = work[:, size:]


def inverse_factor(gram):
    size = gram.shape[0]
    return pl.pallas_call(
        inverse_factor_kernel,
        out_shape=jax.ShapeDtypeStruct((size, size), F32),
        in_specs=[pl.BlockSpec(memory_space=pltpu.VMEM)],
        out_specs=pl.BlockSpec(memory_space=pltpu.VMEM),
        scratch_shapes=[
            pltpu.VMEM((size, 2 * size), F32),
            pltpu.VMEM((PANEL, PANEL, BLK), F32),
            pltpu.VMEM((PANEL, BLK), F32),
            pltpu.VMEM((PANEL, BLK), F32),
        ],
        cost_estimate=pl.CostEstimate(flops=2**34, bytes_accessed=2**19, transcendentals=0),
    )(gram)


def quarters(value):
    return [value[None, q * HALF : (q + 1) * HALF] for q in range(4)]


def gather_row(value):
    return sum([gather(part, steps) for part, steps in zip(quarters(value), ROW_STEPS)], [])


def gather_two(value, steps):
    return jnp.concatenate(gather(value, steps[:2]))


def scatter_row(outs):
    parts = [scatter(outs[2 * q], outs[2 * q + 1], ROW_STEPS[q])[0] for q in range(4)]
    return jnp.concatenate(parts, axis=0)


def scatter_col(keep, send):
    got = flip(send, CORE)
    parts = []
    for half, steps in enumerate(COL_STEPS):
        low, high = slice(4 * half, 4 * half + 2), slice(4 * half + 2, 4 * half + 4)
        parts.append(scatter(keep[low] + got[low], keep[high] + got[high], steps)[0])
    return parts


def gather_col(value):
    pieces = []
    for half, steps in enumerate(COL_STEPS):
        pieces += gather(value[None, half * BLK : (half + 1) * BLK], steps)
    return pieces + [flip(piece, CORE) for piece in pieces]


def gram_sum(gram):
    half = gram.shape[0] // 2
    core = lax.axis_index("c")
    kept = lax.dynamic_slice_in_dim(gram, core * half, half, 0)
    sent = lax.dynamic_slice_in_dim(gram, (1 - core) * half, half, 0)
    value = kept + flip(sent, CORE)
    for axis in "xyz":
        value = ring_sum(value, axis)
    other = flip(value, CORE)
    return jnp.where(
        core == 0, jnp.concatenate([value, other]), jnp.concatenate([other, value])
    )


def local(trial_vectors, tiles, tile_rows, tile_cols, tile_count):
    x, y, z, core = [lax.axis_index(a) for a in ("x", "y", "z", "c")]
    slots = tiles.shape[2]
    width = trial_vectors.shape[1]
    tiles = tiles.reshape(slots, BLK, BLK)
    count = tile_count.reshape(1)

    row = tile_rows.reshape(slots)
    col = tile_cols.reshape(slots)
    near, far = flip_bits(z, row // 4)
    slab = (((row // 2) % 2) ^ core) * 8 + jnp.where(row % 2 == 0, near + 2 * far, 4 + far + 2 * near)
    near_x, far_x = flip_bits(x, col // 8)
    near_y, far_y = flip_bits(y, (col // 2) % 4)
    at_x, at_y = near_x + 2 * far_x, near_y + 2 * far_y
    member = jnp.where(col % 2 == 0, at_x + 4 * at_y, 16 + at_y + 4 * at_x)
    put_first = jnp.concatenate([slab * (BLK + 8), slab])
    put_later = slab * BLK
    put_backward = member * BLK

    begun = [gather_two(part, steps) for part, steps in zip(quarters(trial_vectors), ROW_STEPS)]
    pieces = sum([gather(part, steps[2:]) for part, steps in zip(begun, ROW_STEPS)], [])

    sums = rowsum_call(
        count, (slab // 8) * 8 + (near + 2 * far) * 2 + row % 2, tiles, 16, begun
    ).reshape(2, 2, 2, 2, BLK)
    got = sums[0] + flip(sums[1], CORE)
    inverse_own = 1.0 / (1.0 + scatter(got[0], got[1], COL_STEPS[0])[0])
    gathered = jnp.concatenate(gather(inverse_own[None], ROW_STEPS[0]))
    inverse = jnp.concatenate(
        [gathered[:, 0], gathered[:, 1].reshape(4, 4, BLK).swapaxes(0, 1).reshape(16, BLK)]
    )
    inverse_own = inverse_own.reshape(2 * BLK, 1)

    vectors = trial_vectors
    factor = None
    scale = None
    for iteration in range(ITERS):
        keep, send = forward_call(
            count,
            put_first if iteration == 0 else put_later,
            member,
            tiles,
            inverse,
            factor,
            pieces,
        )
        one, two = scatter_col(keep, send)
        if iteration == 0:
            tilde = jnp.concatenate([one[BLK, :BLK], two[BLK, :BLK]]).reshape(2 * BLK, 1)
            scale = inverse_own / (inverse_own * (inverse_own + tilde))
        summed = jnp.concatenate([one[:BLK], two[:BLK]])
        weighted = scale * (scale * (summed + inverse_own * vectors))
        outs = backward_call(count, put_backward, slab, tiles, gather_col(weighted))
        reduced = inverse_own * (scatter_row(outs) + weighted)
        gram = lax.dot_general(
            reduced,
            reduced,
            (((0,), (0,)), ((), ())),
            precision=HIGHEST,
            preferred_element_type=F32,
        )
        if iteration + 1 < ITERS:
            pieces = gather_row(reduced)
        factor = inverse_factor(gram_sum(gram))
        vectors = nt_dot(reduced, factor)
    total_nodes = 2 * BLK * 128
    return vectors * math.sqrt(total_nodes)


def solution(mesh):
    fine = Mesh(mesh.devices.reshape(4, 4, 4, 2), ("x", "y", "z", "c"))
    row, column = ("x", "y"), ("z", "c")
    in_specs = (
        P(row + column, None),
        P(row, column, None, None, None),
        P(row, column, None),
        P(row, column, None),
        P(row, column),
    )
    return jax.shard_map(
        local, mesh=fine, in_specs=in_specs, out_specs=P(row + column, None), check_vma=False
    )
```

```python
import functools
import math

import jax
import jax.numpy as jnp
from jax import lax
from jax.experimental import pallas as pl
from jax.experimental.pallas import tpu as pltpu
from jax.sharding import Mesh
from jax.sharding import PartitionSpec as P

ITERS = 2
HIGHEST = lax.Precision.HIGHEST
F32 = jnp.float32
BF16 = jnp.bfloat16
BLK = 128
HALF = 64
CHUNK = 32
UNROLL = 16


def flip(value, step):
    axis, mask = step
    return lax.ppermute(value, axis, [(i, i ^ mask) for i in range(2 if axis == "c" else 4)])


def gather(value, steps):
    for step in steps[:-1]:
        value = jnp.concatenate([value, flip(value, step)])
    return [value, flip(value, steps[-1])]


def scatter(keep, send, steps):
    for step in reversed(steps[1:]):
        got = flip(send, step)
        half = keep.shape[0] // 2
        keep, send = keep[:half] + got[:half], keep[half:] + got[half:]
    return keep + flip(send, steps[0])


X1, X3, Y1, Y3, Z1, Z3 = [(axis, mask) for axis in "xyz" for mask in (1, 3)]
CORE = ("c", 1)
LIGHT = [[X1, X3], [Y1, Y3]]
HEAVY = [[Y1, Y3], [Y3, Y1], [X1, X3], [X3, X1]]
COL_STEPS = [[Z1, Z3], [Z3, Z1]]


def flip_bits(mine, other):
    offset = mine ^ other
    return jnp.where((offset == 1) | (offset == 2), 1, 0), jnp.where(offset >= 2, 1, 0)


def swapped(index):
    return (index & 3) + (index & 4) * 2 + (index & 8) // 2


def split(value):
    high = value.astype(BF16)
    return high, (value - high.astype(F32)).astype(BF16)


def nt_dot(a, b, precision=HIGHEST):
    return lax.dot_general(
        a, b, (((1,), (1,)), ((), ())), precision=precision, preferred_element_type=F32
    )


def lane_sums(total):
    lanes = total.shape[-1]
    return nt_dot(jnp.ones((8, lanes), F32), total[...].reshape(-1, lanes))[0:1, :]


def live_tile(tiles_ref, slot, first, count):
    return jnp.where(first + slot < count, tiles_ref[slot], 0.0)


def rowsum_kernel(count_ref, put_ref, tiles_ref, *refs):
    out_ref, total = refs[-2:]
    step = pl.program_id(0)
    count = count_ref[0]

    @pl.when(step == 0)
    def _():
        total[...] = jnp.zeros_like(total)

    first = step * CHUNK

    @pl.when(first < count)
    def _():
        def one(slot, carry):
            block = put_ref[first + slot]
            total[block] += live_tile(tiles_ref, slot, first, count)
            return carry

        lax.fori_loop(0, CHUNK, one, 0, unroll=UNROLL)

    @pl.when(step == pl.num_programs(0) - 1)
    def _():
        out_ref[...] = lane_sums(total)


def chunk_map(step, count_ref, *_):
    return (jnp.minimum(step, (count_ref[0] + CHUNK - 1) // CHUNK - 1), 0, 0)


def rowsum_call(count, put, tiles, out_blocks, after):
    slots = tiles.shape[0]
    return pl.pallas_call(
        rowsum_kernel,
        out_shape=jax.ShapeDtypeStruct((1, out_blocks * BLK), F32),
        grid_spec=pltpu.PrefetchScalarGridSpec(
            num_scalar_prefetch=2,
            grid=(slots // CHUNK,),
            in_specs=[pl.BlockSpec((CHUNK, BLK, BLK), chunk_map)]
            + [pl.BlockSpec(memory_space=pl.ANY)] * len(after),
            out_specs=pl.BlockSpec((1, out_blocks * BLK), lambda s, *_: (0, 0)),
            scratch_shapes=[pltpu.VMEM((out_blocks, BLK, BLK), F32)],
        ),
        cost_estimate=pl.CostEstimate(flops=10**10, bytes_accessed=2**23, transcendentals=0),
    )(count, put, tiles, *after)


def apply_loop(
    count, first, put_ref, take_ref, tiles_ref, source, total, adjoint, tilde, inverse_ref
):
    def one(slot, carry):
        tile = live_tile(tiles_ref, slot, first, count)
        take = take_ref[first + slot]
        put = pl.multiple_of(put_ref[first + slot], 8)
        if tilde is not None:
            tilde_block = put_ref[put_ref.shape[0] // 2 + first + slot]
            tilde[tilde_block] += tile * inverse_ref[pl.ds(take, 1), :]
        if adjoint:
            tile = tile.T
        high, low = split(tile)
        product = jnp.dot(
            jnp.concatenate([high, high], axis=1), source[take], preferred_element_type=F32
        ) + jnp.dot(low, source[take, :BLK], preferred_element_type=F32)
        total[pl.ds(put, BLK), :] += product
        return carry

    lax.fori_loop(0, CHUNK, one, 0, unroll=UNROLL)


def put_source(source, index, row, value):
    high, low = split(value)
    rows = value.shape[0]
    source[index, row : row + rows] = high
    source[index, BLK + row : BLK + row + rows] = low


def piece_place(quarter, index):
    place = index if quarter % 2 == 0 else swapped(index)
    return (quarter // 2) * 16 + place, (quarter % 2) * HALF


def forward_kernel(first_pass, *refs):
    count_ref, put_ref, take_ref, tiles_ref, inverse_ref = refs[:5]
    factor_ref = None
    refs = refs[5:]
    if not first_pass:
        factor_ref, refs = refs[0], refs[1:]
    pieces, targets, refs = refs[:8], refs[8:10], refs[10:]
    source, total = refs[:2]
    tilde = refs[2] if first_pass else None
    step = pl.program_id(0)
    count = count_ref[0]
    first = step * CHUNK

    @pl.when(step == 0)
    def _():
        total[...] = jnp.zeros_like(total)
        if first_pass:
            tilde[...] = jnp.zeros_like(tilde)
        inverse = inverse_ref[...].T
        for number, piece in enumerate(pieces):
            quarter, half = number // 2, number % 2
            if not first_pass:
                values = nt_dot(piece[...].reshape(8 * HALF, -1), factor_ref[...])
            for part in range(8):
                index, row = piece_place(quarter, half * 8 + part)
                value = piece[part] if first_pass else values[part * HALF : (part + 1) * HALF]
                put_source(source, index, row, value * inverse[row : row + HALF, index : index + 1])

    @pl.when(first < count)
    def _():
        apply_loop(
            count, first, put_ref, take_ref, tiles_ref, source, total, False, tilde, inverse_ref
        )

    @pl.when(step == pl.num_programs(0) - 1)
    def _():
        rows = targets[0].shape[1]
        lines = lane_sums(tilde) if first_pass else None
        for number in range(16):
            if first_pass:
                line = lines[:, number * BLK : (number + 1) * BLK]
                total[number * rows + BLK : (number + 1) * rows, :BLK] = jnp.broadcast_to(
                    line, (rows - BLK, BLK)
                )
            targets[number // 8][number % 8] = total[number * rows : (number + 1) * rows, :]


def whole(shape):
    return pl.BlockSpec(shape, lambda s, *_: (0,) * len(shape), pipeline_mode=pl.Buffered(1))


def forward_call(count, put, take, tiles, inverse, factor, pieces):
    first_pass = factor is None
    slots = tiles.shape[0]
    width = pieces[0].shape[-1]
    rows = BLK + (8 if first_pass else 0)
    extra = [] if first_pass else [factor]
    out = jax.ShapeDtypeStruct((8, rows, width), F32)
    scratch = [pltpu.VMEM((32, 2 * BLK, width), BF16), pltpu.VMEM((16 * rows, width), F32)]
    if first_pass:
        scratch.append(pltpu.VMEM((16, BLK, BLK), F32))
    return pl.pallas_call(
        functools.partial(forward_kernel, first_pass),
        out_shape=(out,) * 2,
        grid_spec=pltpu.PrefetchScalarGridSpec(
            num_scalar_prefetch=3,
            grid=(slots // CHUNK,),
            in_specs=[pl.BlockSpec((CHUNK, BLK, BLK), chunk_map)]
            + [whole(a.shape) for a in [inverse] + extra + list(pieces)],
            out_specs=(whole(out.shape),) * 2,
            scratch_shapes=scratch,
        ),
        cost_estimate=pl.CostEstimate(
            flops=6 * 2**30, bytes_accessed=2**24, transcendentals=0
        ),
    )(count, put, take, tiles, inverse, *extra, *pieces)


def backward_kernel(*refs):
    count_ref, put_ref, take_ref, tiles_ref = refs[:4]
    pieces, outs, (source, total) = refs[4:12], refs[12:20], refs[20:]
    step = pl.program_id(0)
    count = count_ref[0]
    first = step * CHUNK

    @pl.when(step == 0)
    def _():
        total[...] = jnp.zeros_like(total)
        for number, piece in enumerate(pieces):
            for part in range(2):
                put_source(source, number * 2 + part, 0, piece[part])

    @pl.when(first < count)
    def _():
        apply_loop(count, first, put_ref, take_ref, tiles_ref, source, total, True, None, None)

    @pl.when(step == pl.num_programs(0) - 1)
    def _():
        for number, out in enumerate(outs):
            for part in range(8):
                index, row = piece_place(number // 2, number % 2 * 8 + part)
                out[part] = total[index * BLK + row : index * BLK + row + HALF, :]


def backward_call(count, put, take, tiles, pieces):
    slots = tiles.shape[0]
    width = pieces[0].shape[-1]
    out = jax.ShapeDtypeStruct((8, HALF, width), F32)
    return pl.pallas_call(
        backward_kernel,
        out_shape=(out,) * 8,
        grid_spec=pltpu.PrefetchScalarGridSpec(
            num_scalar_prefetch=3,
            grid=(slots // CHUNK,),
            in_specs=[pl.BlockSpec((CHUNK, BLK, BLK), chunk_map)]
            + [whole(a.shape) for a in pieces],
            out_specs=(whole(out.shape),) * 8,
            scratch_shapes=[
                pltpu.VMEM((16, 2 * BLK, width), BF16),
                pltpu.VMEM((32 * BLK, width), F32),
            ],
        ),
        cost_estimate=pl.CostEstimate(
            flops=6 * 2**30, bytes_accessed=2**24, transcendentals=0
        ),
    )(count, put, take, tiles, *pieces)


PANEL = 32


def inverse_factor_kernel(one_ref, two_ref, out_ref, work, columns, multiplier, right):
    size = out_ref.shape[0]
    lanes = columns.shape[-1]
    half, quarter = size // 2, size // 4
    work[:half, :half] = one_ref[:half]
    work[:quarter, half:size] = one_ref[half:]
    work[quarter:half, half:size] = two_ref[:quarter]
    work[half:, half:size] = two_ref[quarter:]
    work[half:, :half] = jnp.zeros((half, half), F32)
    row_at = lax.broadcasted_iota(jnp.int32, (size, size), 0)
    lane_at = lax.broadcasted_iota(jnp.int32, (size, size), 1)
    work[:, size:] = (row_at == lane_at).astype(F32)
    row_small = lax.broadcasted_iota(jnp.int32, (PANEL, lanes), 0)
    lane_small = lax.broadcasted_iota(jnp.int32, (PANEL, lanes), 1)
    unit = (row_small == lane_small).astype(F32)
    for start in range(0, size, PANEL):
        end = start + PANEL
        corner = work[start:end, start:end]
        for k in range(PANEL):
            columns[k] = jnp.broadcast_to(corner[:, k : k + 1], (PANEL, lanes))
        right[...] = unit
        for j in range(PANEL - 1):
            low = 8 * ((j + 1) // 8)
            column = columns[j, low:, :]
            factor = jnp.where(row_small[low:] > j, column, 0.0) * (1.0 / columns[j, j : j + 1, :])
            multiplier[low:, :] = factor
            for k in range(j + 1, PANEL):
                k_low = 8 * (k // 8)
                columns[k, k_low:, :] -= column[k_low - low :] * multiplier[k : k + 1, :]
            right[low:, :] -= factor * right[j : j + 1, :]
        pivots = jnp.concatenate([columns[k, k : k + 1, :] for k in range(PANEL)], axis=0)
        corner = (right[...] * (1.0 / jnp.sqrt(pivots)))[:, :PANEL]
        left = lanes * (start // lanes)
        used = size + lanes * ((end + lanes - 1) // lanes)
        panel = jnp.dot(
            corner, work[start:end, left:used], precision=HIGHEST, preferred_element_type=F32
        )
        work[start:end, left:used] = panel
        if end < size:
            update = lax.dot_general(
                panel[:, : size - left],
                panel,
                (((0,), (0,)), ((), ())),
                precision=HIGHEST,
                preferred_element_type=F32,
            )
            work[end:, left:used] -= update[end - left :, :]
    out_ref[...] = work[:, size:]


def inverse_factor(one, two):
    size = 2 * one.shape[1]
    return pl.pallas_call(
        inverse_factor_kernel,
        out_shape=jax.ShapeDtypeStruct((size, size), F32),
        in_specs=[pl.BlockSpec(memory_space=pltpu.VMEM)] * 2,
        out_specs=pl.BlockSpec(memory_space=pltpu.VMEM),
        scratch_shapes=[
            pltpu.VMEM((size, 2 * size), F32),
            pltpu.VMEM((PANEL, PANEL, BLK), F32),
            pltpu.VMEM((PANEL, BLK), F32),
            pltpu.VMEM((PANEL, BLK), F32),
        ],
        cost_estimate=pl.CostEstimate(flops=2**34, bytes_accessed=2**19, transcendentals=0),
    )(one, two)


def gather_light(value):
    return [
        jnp.concatenate(gather(value[None, half * BLK : (half + 1) * BLK], LIGHT[half]))
        for half in range(2)
    ]


def gather_heavy(halves):
    pieces = []
    for number, steps in enumerate(HEAVY):
        row = number % 2 * HALF
        pieces += gather(halves[number // 2][:, row : row + HALF], steps)
    return pieces


def scatter_row(outs):
    parts = []
    for half in range(2):
        pair = [
            scatter(outs[2 * number], outs[2 * number + 1], HEAVY[number])
            for number in (2 * half, 2 * half + 1)
        ]
        pair = jnp.concatenate(pair, axis=1)
        parts.append(scatter(pair[:2], pair[2:], LIGHT[half])[0])
    return jnp.concatenate(parts, axis=0)


def scatter_col(keep, send):
    got = flip(send, CORE)
    parts = []
    for half, steps in enumerate(COL_STEPS):
        low, high = slice(4 * half, 4 * half + 2), slice(4 * half + 2, 4 * half + 4)
        parts.append(scatter(keep[low] + got[low], keep[high] + got[high], steps)[0])
    return parts


def gather_col(value):
    pieces = []
    for half, steps in enumerate(COL_STEPS):
        pieces += gather(value[None, half * BLK : (half + 1) * BLK], steps)
    return pieces + [flip(piece, CORE) for piece in pieces]


def gram_sum(gram):
    half = gram.shape[0] // 2
    core = lax.axis_index("c")
    halves = [
        jnp.concatenate([gram[:half, :half], gram[: half // 2, half:]]),
        jnp.concatenate([gram[half // 2 : half, half:], gram[half:, half:]]),
    ]
    value = jnp.where(core == 0, *halves) + flip(jnp.where(core == 0, *halves[::-1]), CORE)
    for step in (X1, X3, Y1, Y3, Z1, Z3):
        value = value + flip(value, step)
    other = flip(value, CORE)
    return jnp.where(core == 0, value, other), jnp.where(core == 0, other, value)


def local(trial_vectors, tiles, tile_rows, tile_cols, tile_count):
    x, y, z, core = [lax.axis_index(a) for a in ("x", "y", "z", "c")]
    slots = tiles.shape[2]
    width = trial_vectors.shape[1]
    tiles = tiles.reshape(slots, BLK, BLK)
    count = tile_count.reshape(1)

    row = tile_rows.reshape(slots)
    col = tile_cols.reshape(slots)
    near, far = flip_bits(z, row // 4)
    part = row % 2
    slab = ((row // 2) % 2 ^ core) * 8 + jnp.where(part == 0, near + 2 * far, 4 + far + 2 * near)
    near_x, far_x = flip_bits(x, col // 8)
    near_y, far_y = flip_bits(y, (col // 2) % 4)
    at_x, at_y = near_x + 2 * far_x, near_y + 2 * far_y
    member = jnp.where(col % 2 == 0, at_x + 4 * at_y, 16 + at_y + 4 * at_x)
    put_first = jnp.concatenate([slab * (BLK + 8), slab])
    put_later = slab * BLK
    put_backward = member * BLK

    begun = gather_light(trial_vectors)
    pieces = gather_heavy(begun)

    sums = rowsum_call(
        count, (slab // 8) * 8 + (near + 2 * far) * 2 + part, tiles, 16, begun
    ).reshape(2, 2, 2, 2, BLK)
    got = sums[0] + flip(sums[1], CORE)
    inverse_own = 1.0 / (1.0 + scatter(got[0], got[1], COL_STEPS[0])[0])
    gathered = jnp.concatenate(gather(inverse_own[None], LIGHT[0] + LIGHT[1]))
    inverse = jnp.concatenate(
        [gathered[:, 0], gathered[:, 1].reshape(4, 4, BLK).swapaxes(0, 1).reshape(16, BLK)]
    )
    inverse_own = inverse_own.reshape(2 * BLK, 1)

    vectors = trial_vectors
    factor = None
    scale = None
    for iteration in range(ITERS):
        outs = forward_call(
            count,
            put_first if iteration == 0 else put_later,
            member,
            tiles,
            inverse,
            factor,
            pieces,
        )
        one, two = scatter_col(*outs)
        if iteration == 0:
            tilde = jnp.concatenate([one[BLK, :BLK], two[BLK, :BLK]]).reshape(2 * BLK, 1)
            scale = inverse_own / (inverse_own * (inverse_own + tilde))
        summed = jnp.concatenate([one[:BLK], two[:BLK]])
        weighted = scale * (scale * (summed + inverse_own * vectors))
        outs = backward_call(count, put_backward, slab, tiles, gather_col(weighted))
        reduced = inverse_own * (scatter_row(outs) + weighted)
        gram = lax.dot_general(
            reduced,
            reduced,
            (((0,), (0,)), ((), ())),
            precision=HIGHEST,
            preferred_element_type=F32,
        )
        if iteration + 1 < ITERS:
            pieces = gather_heavy(gather_light(reduced))
        factor = inverse_factor(*gram_sum(gram))
        vectors = nt_dot(reduced, factor)
    total_nodes = 2 * BLK * 128
    return vectors * math.sqrt(total_nodes)


def solution(mesh):
    fine = Mesh(mesh.devices.reshape(4, 4, 4, 2), ("x", "y", "z", "c"))
    row, column = ("x", "y"), ("z", "c")
    in_specs = (
        P(row + column, None),
        P(row, column, None, None, None),
        P(row, column, None),
        P(row, column, None),
        P(row, column),
    )
    return jax.shard_map(
        local, mesh=fine, in_specs=in_specs, out_specs=P(row + column, None), check_vma=False
    )
```

```python
import functools
import math

import jax
import jax.numpy as jnp
from jax import lax
from jax.experimental import pallas as pl
from jax.experimental.pallas import tpu as pltpu
from jax.sharding import Mesh
from jax.sharding import PartitionSpec as P

ITERS = 2
HIGHEST = lax.Precision.HIGHEST
F32 = jnp.float32
BF16 = jnp.bfloat16
BLK = 128
HALF = 64
CHUNK = 32
UNROLL = 16


def flip(value, step):
    axis, mask = step
    return lax.ppermute(value, axis, [(i, i ^ mask) for i in range(2 if axis == "c" else 4)])


def gather(value, steps):
    for step in steps[:-1]:
        value = jnp.concatenate([value, flip(value, step)])
    return [value, flip(value, steps[-1])]


def scatter(keep, send, steps):
    for step in reversed(steps[1:]):
        got = flip(send, step)
        half = keep.shape[0] // 2
        keep, send = keep[:half] + got[:half], keep[half:] + got[half:]
    return keep + flip(send, steps[0])


X1, X3, Y1, Y3, Z1, Z3 = [(axis, mask) for axis in "xyz" for mask in (1, 3)]
CORE = ("c", 1)
LIGHT = [[X1, X3], [Y1, Y3]]
HEAVY = [[Y1, Y3], [Y3, Y1], [X1, X3], [X3, X1]]
COL_STEPS = [[Z1, Z3], [Z3, Z1]]


def flip_bits(mine, other):
    offset = mine ^ other
    return jnp.where((offset == 1) | (offset == 2), 1, 0), jnp.where(offset >= 2, 1, 0)


def swapped(index):
    return (index & 3) + (index & 4) * 2 + (index & 8) // 2


def split(value):
    high = value.astype(BF16)
    return high, (value - high.astype(F32)).astype(BF16)


def nt_dot(a, b, precision=HIGHEST):
    return lax.dot_general(
        a, b, (((1,), (1,)), ((), ())), precision=precision, preferred_element_type=F32
    )


def lane_sums(total):
    lanes = total.shape[-1]
    return nt_dot(jnp.ones((8, lanes), F32), total[...].reshape(-1, lanes))[0:1, :]


def live_tile(tiles_ref, slot, first, count):
    return jnp.where(first + slot < count, tiles_ref[slot], 0.0)


def rowsum_kernel(count_ref, put_ref, tiles_ref, *refs):
    out_ref, total = refs[-2:]
    step = pl.program_id(0)
    count = count_ref[0]

    @pl.when(step == 0)
    def _():
        total[...] = jnp.zeros_like(total)

    first = step * CHUNK

    @pl.when(first < count)
    def _():
        def one(slot, carry):
            block = put_ref[first + slot]
            total[block] += live_tile(tiles_ref, slot, first, count)
            return carry

        lax.fori_loop(0, CHUNK, one, 0, unroll=UNROLL)

    @pl.when(step == pl.num_programs(0) - 1)
    def _():
        out_ref[...] = lane_sums(total)


def chunk_map(step, count_ref, *_):
    return (jnp.minimum(step, (count_ref[0] + CHUNK - 1) // CHUNK - 1), 0, 0)


def rowsum_call(count, put, tiles, out_blocks, after):
    slots = tiles.shape[0]
    return pl.pallas_call(
        rowsum_kernel,
        out_shape=jax.ShapeDtypeStruct((1, out_blocks * BLK), F32),
        grid_spec=pltpu.PrefetchScalarGridSpec(
            num_scalar_prefetch=2,
            grid=(slots // CHUNK,),
            in_specs=[pl.BlockSpec((CHUNK, BLK, BLK), chunk_map)]
            + [pl.BlockSpec(memory_space=pl.ANY)] * len(after),
            out_specs=pl.BlockSpec((1, out_blocks * BLK), lambda s, *_: (0, 0)),
            scratch_shapes=[pltpu.VMEM((out_blocks, BLK, BLK), F32)],
        ),
        compiler_params=pltpu.CompilerParams(vmem_limit_bytes=12 * 2**20),
        cost_estimate=pl.CostEstimate(flops=10**10, bytes_accessed=2**23, transcendentals=0),
    )(count, put, tiles, *after)


def apply_loop(
    count, first, put_ref, take_ref, tiles_ref, source, total, adjoint, tilde, inverse_ref
):
    def one(slot, carry):
        tile = live_tile(tiles_ref, slot, first, count)
        take = take_ref[first + slot]
        put = pl.multiple_of(put_ref[first + slot], 8)
        if tilde is not None:
            tilde_block = put_ref[put_ref.shape[0] // 2 + first + slot]
            tilde[tilde_block] += tile * inverse_ref[pl.ds(take, 1), :]
        if adjoint:
            tile = tile.T
        high, low = split(tile)
        product = jnp.dot(
            jnp.concatenate([high, high], axis=1), source[take], preferred_element_type=F32
        ) + jnp.dot(low, source[take, :BLK], preferred_element_type=F32)
        total[pl.ds(put, BLK), :] += product
        return carry

    lax.fori_loop(0, CHUNK, one, 0, unroll=UNROLL)


def put_source(source, index, row, value):
    high, low = split(value)
    rows = value.shape[0]
    source[index, row : row + rows] = high
    source[index, BLK + row : BLK + row + rows] = low


def piece_place(quarter, index):
    place = index if quarter % 2 == 0 else swapped(index)
    return (quarter // 2) * 16 + place, (quarter % 2) * HALF


def forward_kernel(first_pass, *refs):
    count_ref, put_ref, take_ref, tiles_ref, inverse_ref = refs[:5]
    factor_ref = None
    refs = refs[5:]
    if not first_pass:
        factor_ref, refs = refs[0], refs[1:]
    pieces, targets, refs = refs[:8], refs[8:10], refs[10:]
    source, total = refs[:2]
    tilde = refs[2] if first_pass else None
    step = pl.program_id(0)
    count = count_ref[0]
    first = step * CHUNK

    @pl.when(step == 0)
    def _():
        total[...] = jnp.zeros_like(total)
        if first_pass:
            tilde[...] = jnp.zeros_like(tilde)
        inverse = inverse_ref[...].T
        for number, piece in enumerate(pieces):
            quarter, half = number // 2, number % 2
            if not first_pass:
                values = nt_dot(piece[...].reshape(8 * HALF, -1), factor_ref[...])
            for part in range(8):
                index, row = piece_place(quarter, half * 8 + part)
                value = piece[part] if first_pass else values[part * HALF : (part + 1) * HALF]
                put_source(source, index, row, value * inverse[row : row + HALF, index : index + 1])

    @pl.when(first < count)
    def _():
        apply_loop(
            count, first, put_ref, take_ref, tiles_ref, source, total, False, tilde, inverse_ref
        )

    @pl.when(step == pl.num_programs(0) - 1)
    def _():
        rows = targets[0].shape[1]
        lines = lane_sums(tilde) if first_pass else None
        for number in range(16):
            if first_pass:
                line = lines[:, number * BLK : (number + 1) * BLK]
                total[number * rows + BLK : (number + 1) * rows, :BLK] = jnp.broadcast_to(
                    line, (rows - BLK, BLK)
                )
            targets[number // 8][number % 8] = total[number * rows : (number + 1) * rows, :]


def whole(shape):
    return pl.BlockSpec(shape, lambda s, *_: (0,) * len(shape), pipeline_mode=pl.Buffered(1))


def forward_call(count, put, take, tiles, inverse, factor, pieces):
    first_pass = factor is None
    slots = tiles.shape[0]
    width = pieces[0].shape[-1]
    rows = BLK + (8 if first_pass else 0)
    extra = [] if first_pass else [factor]
    out = jax.ShapeDtypeStruct((8, rows, width), F32)
    scratch = [pltpu.VMEM((32, 2 * BLK, width), BF16), pltpu.VMEM((16 * rows, width), F32)]
    if first_pass:
        scratch.append(pltpu.VMEM((16, BLK, BLK), F32))
    return pl.pallas_call(
        functools.partial(forward_kernel, first_pass),
        out_shape=(out,) * 2,
        grid_spec=pltpu.PrefetchScalarGridSpec(
            num_scalar_prefetch=3,
            grid=(slots // CHUNK,),
            in_specs=[pl.BlockSpec((CHUNK, BLK, BLK), chunk_map)]
            + [whole(a.shape) for a in [inverse] + extra + list(pieces)],
            out_specs=(whole(out.shape),) * 2,
            scratch_shapes=scratch,
        ),
        compiler_params=pltpu.CompilerParams(vmem_limit_bytes=26 * 2**20),
        cost_estimate=pl.CostEstimate(
            flops=6 * 2**30, bytes_accessed=2**24, transcendentals=0
        ),
    )(count, put, take, tiles, inverse, *extra, *pieces)


def backward_kernel(*refs):
    count_ref, put_ref, take_ref, tiles_ref = refs[:4]
    pieces, outs, (source, total) = refs[4:12], refs[12:20], refs[20:]
    step = pl.program_id(0)
    count = count_ref[0]
    first = step * CHUNK

    @pl.when(step == 0)
    def _():
        total[...] = jnp.zeros_like(total)
        for number, piece in enumerate(pieces):
            for part in range(2):
                put_source(source, number * 2 + part, 0, piece[part])

    @pl.when(first < count)
    def _():
        apply_loop(count, first, put_ref, take_ref, tiles_ref, source, total, True, None, None)

    @pl.when(step == pl.num_programs(0) - 1)
    def _():
        for number, out in enumerate(outs):
            for part in range(8):
                index, row = piece_place(number // 2, number % 2 * 8 + part)
                out[part] = total[index * BLK + row : index * BLK + row + HALF, :]


def backward_call(count, put, take, tiles, pieces):
    slots = tiles.shape[0]
    width = pieces[0].shape[-1]
    out = jax.ShapeDtypeStruct((8, HALF, width), F32)
    return pl.pallas_call(
        backward_kernel,
        out_shape=(out,) * 8,
        grid_spec=pltpu.PrefetchScalarGridSpec(
            num_scalar_prefetch=3,
            grid=(slots // CHUNK,),
            in_specs=[pl.BlockSpec((CHUNK, BLK, BLK), chunk_map)]
            + [whole(a.shape) for a in pieces],
            out_specs=(whole(out.shape),) * 8,
            scratch_shapes=[
                pltpu.VMEM((16, 2 * BLK, width), BF16),
                pltpu.VMEM((32 * BLK, width), F32),
            ],
        ),
        compiler_params=pltpu.CompilerParams(vmem_limit_bytes=26 * 2**20),
        cost_estimate=pl.CostEstimate(
            flops=6 * 2**30, bytes_accessed=2**24, transcendentals=0
        ),
    )(count, put, take, tiles, *pieces)


PANEL = 32


def inverse_factor_kernel(one_ref, two_ref, out_ref, work, columns, multiplier, right):
    size = out_ref.shape[0]
    lanes = columns.shape[-1]
    half, quarter = size // 2, size // 4
    work[:half, :half] = one_ref[:half]
    work[:quarter, half:size] = one_ref[half:]
    work[quarter:half, half:size] = two_ref[:quarter]
    work[half:, half:size] = two_ref[quarter:]
    work[half:, :half] = jnp.zeros((half, half), F32)
    row_at = lax.broadcasted_iota(jnp.int32, (size, size), 0)
    lane_at = lax.broadcasted_iota(jnp.int32, (size, size), 1)
    work[:, size:] = (row_at == lane_at).astype(F32)
    row_small = lax.broadcasted_iota(jnp.int32, (PANEL, lanes), 0)
    lane_small = lax.broadcasted_iota(jnp.int32, (PANEL, lanes), 1)
    unit = (row_small == lane_small).astype(F32)
    for start in range(0, size, PANEL):
        end = start + PANEL
        corner = work[start:end, start:end]
        for k in range(PANEL):
            columns[k] = jnp.broadcast_to(corner[:, k : k + 1], (PANEL, lanes))
        right[...] = unit
        for j in range(PANEL - 1):
            low = 8 * ((j + 1) // 8)
            column = columns[j, low:, :]
            factor = jnp.where(row_small[low:] > j, column, 0.0) * (1.0 / columns[j, j : j + 1, :])
            multiplier[low:, :] = factor
            for k in range(j + 1, PANEL):
                k_low = 8 * (k // 8)
                columns[k, k_low:, :] -= column[k_low - low :] * multiplier[k : k + 1, :]
            right[low:, :] -= factor * right[j : j + 1, :]
        pivots = jnp.concatenate([columns[k, k : k + 1, :] for k in range(PANEL)], axis=0)
        corner = (right[...] * (1.0 / jnp.sqrt(pivots)))[:, :PANEL]
        left = lanes * (start // lanes)
        used = size + lanes * ((end + lanes - 1) // lanes)
        panel = jnp.dot(
            corner, work[start:end, left:used], precision=HIGHEST, preferred_element_type=F32
        )
        work[start:end, left:used] = panel
        if end < size:
            update = lax.dot_general(
                panel[:, : size - left],
                panel,
                (((0,), (0,)), ((), ())),
                precision=HIGHEST,
                preferred_element_type=F32,
            )
            work[end:, left:used] -= update[end - left :, :]
    out_ref[...] = work[:, size:]


def inverse_factor(one, two):
    size = 2 * one.shape[1]
    return pl.pallas_call(
        inverse_factor_kernel,
        out_shape=jax.ShapeDtypeStruct((size, size), F32),
        in_specs=[pl.BlockSpec(memory_space=pltpu.VMEM)] * 2,
        out_specs=pl.BlockSpec(memory_space=pltpu.VMEM),
        scratch_shapes=[
            pltpu.VMEM((size, 2 * size), F32),
            pltpu.VMEM((PANEL, PANEL, BLK), F32),
            pltpu.VMEM((PANEL, BLK), F32),
            pltpu.VMEM((PANEL, BLK), F32),
        ],
        compiler_params=pltpu.CompilerParams(vmem_limit_bytes=12 * 2**20),
        cost_estimate=pl.CostEstimate(flops=2**34, bytes_accessed=2**19, transcendentals=0),
    )(one, two)


def gather_light(value):
    return [
        jnp.concatenate(gather(value[None, half * BLK : (half + 1) * BLK], LIGHT[half]))
        for half in range(2)
    ]


def gather_heavy(halves):
    pieces = []
    for number, steps in enumerate(HEAVY):
        row = number % 2 * HALF
        pieces += gather(halves[number // 2][:, row : row + HALF], steps)
    return pieces


def scatter_row(outs):
    parts = []
    for half in range(2):
        pair = [
            scatter(outs[2 * number], outs[2 * number + 1], HEAVY[number])
            for number in (2 * half, 2 * half + 1)
        ]
        pair = jnp.concatenate(pair, axis=1)
        parts.append(scatter(pair[:2], pair[2:], LIGHT[half])[0])
    return jnp.concatenate(parts, axis=0)


def scatter_col(keep, send):
    got = flip(send, CORE)
    parts = []
    for half, steps in enumerate(COL_STEPS):
        low, high = slice(4 * half, 4 * half + 2), slice(4 * half + 2, 4 * half + 4)
        parts.append(scatter(keep[low] + got[low], keep[high] + got[high], steps)[0])
    return parts


def gather_col(value):
    pieces = []
    for half, steps in enumerate(COL_STEPS):
        pieces += gather(value[None, half * BLK : (half + 1) * BLK], steps)
    return pieces + [flip(piece, CORE) for piece in pieces]


def gram_sum(gram):
    half = gram.shape[0] // 2
    core = lax.axis_index("c")
    halves = [
        jnp.concatenate([gram[:half, :half], gram[: half // 2, half:]]),
        jnp.concatenate([gram[half // 2 : half, half:], gram[half:, half:]]),
    ]
    value = jnp.where(core == 0, *halves) + flip(jnp.where(core == 0, *halves[::-1]), CORE)
    for step in (X1, X3, Y1, Y3, Z1, Z3):
        value = value + flip(value, step)
    other = flip(value, CORE)
    return jnp.where(core == 0, value, other), jnp.where(core == 0, other, value)


def local(trial_vectors, tiles, tile_rows, tile_cols, tile_count):
    x, y, z, core = [lax.axis_index(a) for a in ("x", "y", "z", "c")]
    slots = tiles.shape[2]
    width = trial_vectors.shape[1]
    tiles = tiles.reshape(slots, BLK, BLK)
    count = tile_count.reshape(1)

    row = tile_rows.reshape(slots)
    col = tile_cols.reshape(slots)
    near, far = flip_bits(z, row // 4)
    part = row % 2
    slab = ((row // 2) % 2 ^ core) * 8 + jnp.where(part == 0, near + 2 * far, 4 + far + 2 * near)
    near_x, far_x = flip_bits(x, col // 8)
    near_y, far_y = flip_bits(y, (col // 2) % 4)
    at_x, at_y = near_x + 2 * far_x, near_y + 2 * far_y
    member = jnp.where(col % 2 == 0, at_x + 4 * at_y, 16 + at_y + 4 * at_x)
    put_first = jnp.concatenate([slab * (BLK + 8), slab])
    put_later = slab * BLK
    put_backward = member * BLK

    begun = gather_light(trial_vectors)
    pieces = gather_heavy(begun)

    sums = rowsum_call(
        count, (slab // 8) * 8 + (near + 2 * far) * 2 + part, tiles, 16, begun
    ).reshape(2, 2, 2, 2, BLK)
    got = sums[0] + flip(sums[1], CORE)
    inverse_own = 1.0 / (1.0 + scatter(got[0], got[1], COL_STEPS[0])[0])
    gathered = jnp.concatenate(gather(inverse_own[None], LIGHT[0] + LIGHT[1]))
    inverse = jnp.concatenate(
        [gathered[:, 0], gathered[:, 1].reshape(4, 4, BLK).swapaxes(0, 1).reshape(16, BLK)]
    )
    inverse_own = inverse_own.reshape(2 * BLK, 1)

    vectors = trial_vectors
    factor = None
    scale = None
    for iteration in range(ITERS):
        outs = forward_call(
            count,
            put_first if iteration == 0 else put_later,
            member,
            tiles,
            inverse,
            factor,
            pieces,
        )
        one, two = scatter_col(*outs)
        if iteration == 0:
            tilde = jnp.concatenate([one[BLK, :BLK], two[BLK, :BLK]]).reshape(2 * BLK, 1)
            scale = inverse_own / (inverse_own * (inverse_own + tilde))
        summed = jnp.concatenate([one[:BLK], two[:BLK]])
        weighted = scale * (scale * (summed + inverse_own * vectors))
        outs = backward_call(count, put_backward, slab, tiles, gather_col(weighted))
        reduced = inverse_own * (scatter_row(outs) + weighted)
        gram = lax.dot_general(
            reduced,
            reduced,
            (((0,), (0,)), ((), ())),
            precision=HIGHEST,
            preferred_element_type=F32,
        )
        if iteration + 1 < ITERS:
            pieces = gather_heavy(gather_light(reduced))
        factor = inverse_factor(*gram_sum(gram))
        vectors = nt_dot(reduced, factor)
    total_nodes = 2 * BLK * 128
    return vectors * math.sqrt(total_nodes)


def solution(mesh):
    fine = Mesh(mesh.devices.reshape(4, 4, 4, 2), ("x", "y", "z", "c"))
    row, column = ("x", "y"), ("z", "c")
    in_specs = (
        P(row + column, None),
        P(row, column, None, None, None),
        P(row, column, None),
        P(row, column, None),
        P(row, column),
    )
    return jax.shard_map(
        local, mesh=fine, in_specs=in_specs, out_specs=P(row + column, None), check_vma=False
    )
```

```python
import functools
import math

import jax
import jax.numpy as jnp
from jax import lax
from jax.experimental import pallas as pl
from jax.experimental.pallas import tpu as pltpu
from jax.sharding import Mesh
from jax.sharding import PartitionSpec as P

ITERS = 2
HIGHEST = lax.Precision.HIGHEST
F32 = jnp.float32
BF16 = jnp.bfloat16
BLK = 128
HALF = 64
CHUNK = 16
UNROLL = 16


def flip(value, step):
    axis, mask = step
    return lax.ppermute(value, axis, [(i, i ^ mask) for i in range(2 if axis == "c" else 4)])


def gather(value, steps):
    for step in steps[:-1]:
        value = jnp.concatenate([value, flip(value, step)])
    return [value, flip(value, steps[-1])]


def scatter(keep, send, steps):
    for step in reversed(steps[1:]):
        got = flip(send, step)
        half = keep.shape[0] // 2
        keep, send = keep[:half] + got[:half], keep[half:] + got[half:]
    return keep + flip(send, steps[0])


X1, X3, Y1, Y3, Z1, Z3 = [(axis, mask) for axis in "xyz" for mask in (1, 3)]
CORE = ("c", 1)
LIGHT = [[X1, X3], [Y1, Y3]]
HEAVY = [[Y1, Y3], [Y3, Y1], [X1, X3], [X3, X1]]
COL_STEPS = [[Z1, Z3], [Z3, Z1]]


def flip_bits(mine, other):
    offset = mine ^ other
    return jnp.where((offset == 1) | (offset == 2), 1, 0), jnp.where(offset >= 2, 1, 0)


def swapped(index):
    return (index & 3) + (index & 4) * 2 + (index & 8) // 2


def split(value):
    high = value.astype(BF16)
    return high, (value - high.astype(F32)).astype(BF16)


def nt_dot(a, b, precision=HIGHEST):
    return lax.dot_general(
        a, b, (((1,), (1,)), ((), ())), precision=precision, preferred_element_type=F32
    )


def lane_sums(total):
    lanes = total.shape[-1]
    return nt_dot(jnp.ones((8, lanes), F32), total[...].reshape(-1, lanes))[0:1, :]


def live_tile(tiles_ref, slot, first, count):
    return jnp.where(first + slot < count, tiles_ref[slot], 0.0)


def rowsum_kernel(count_ref, put_ref, tiles_ref, *refs):
    out_ref, total = refs[-2:]
    step = pl.program_id(0)
    count = count_ref[0]

    @pl.when(step == 0)
    def _():
        total[...] = jnp.zeros_like(total)

    first = step * CHUNK

    @pl.when(first < count)
    def _():
        def one(slot, carry):
            block = put_ref[first + slot]
            total[block] += live_tile(tiles_ref, slot, first, count)
            return carry

        lax.fori_loop(0, CHUNK, one, 0, unroll=UNROLL)

    @pl.when(step == pl.num_programs(0) - 1)
    def _():
        out_ref[...] = lane_sums(total)


def chunk_map(step, count_ref, *_):
    return (jnp.minimum(step, (count_ref[0] + CHUNK - 1) // CHUNK - 1), 0, 0)


def rowsum_call(count, put, tiles, out_blocks, after):
    slots = tiles.shape[0]
    return pl.pallas_call(
        rowsum_kernel,
        out_shape=jax.ShapeDtypeStruct((1, out_blocks * BLK), F32),
        grid_spec=pltpu.PrefetchScalarGridSpec(
            num_scalar_prefetch=2,
            grid=(slots // CHUNK,),
            in_specs=[pl.BlockSpec((CHUNK, BLK, BLK), chunk_map)]
            + [pl.BlockSpec(memory_space=pl.ANY)] * len(after),
            out_specs=pl.BlockSpec((1, out_blocks * BLK), lambda s, *_: (0, 0)),
            scratch_shapes=[pltpu.VMEM((out_blocks, BLK, BLK), F32)],
        ),
        compiler_params=pltpu.CompilerParams(vmem_limit_bytes=12 * 2**20),
        cost_estimate=pl.CostEstimate(flops=10**10, bytes_accessed=2**23, transcendentals=0),
    )(count, put, in_hbm(tiles), *after)


def apply_loop(
    count, first, put_ref, take_ref, tiles_ref, source, total, adjoint, tilde, inverse_ref
):
    def one(slot, carry):
        tile = live_tile(tiles_ref, slot, first, count)
        take = take_ref[first + slot]
        put = pl.multiple_of(put_ref[first + slot], 8)
        if tilde is not None:
            tilde_block = put_ref[put_ref.shape[0] // 2 + first + slot]
            tilde[tilde_block] += tile * inverse_ref[pl.ds(take, 1), :]
        if adjoint:
            tile = tile.T
        high, low = split(tile)
        product = jnp.dot(
            jnp.concatenate([high, high], axis=1), source[take], preferred_element_type=F32
        ) + jnp.dot(low, source[take, :BLK], preferred_element_type=F32)
        total[pl.ds(put, BLK), :] += product
        return carry

    lax.fori_loop(0, CHUNK, one, 0, unroll=UNROLL)


def put_source(source, index, row, value):
    high, low = split(value)
    rows = value.shape[0]
    source[index, row : row + rows] = high
    source[index, BLK + row : BLK + row + rows] = low


def piece_place(quarter, index):
    place = index if quarter % 2 == 0 else swapped(index)
    return (quarter // 2) * 16 + place, (quarter % 2) * HALF


def forward_kernel(first_pass, *refs):
    count_ref, put_ref, take_ref, tiles_ref, inverse_ref = refs[:5]
    factor_ref = None
    refs = refs[5:]
    if not first_pass:
        factor_ref, refs = refs[0], refs[1:]
    pieces, targets, refs = refs[:8], refs[8:10], refs[10:]
    source, total = refs[:2]
    tilde = refs[2] if first_pass else None
    step = pl.program_id(0)
    count = count_ref[0]
    first = step * CHUNK

    @pl.when(step == 0)
    def _():
        total[...] = jnp.zeros_like(total)
        if first_pass:
            tilde[...] = jnp.zeros_like(tilde)
        inverse = inverse_ref[...].T
        for number, piece in enumerate(pieces):
            quarter, half = number // 2, number % 2
            if not first_pass:
                values = nt_dot(piece[...].reshape(8 * HALF, -1), factor_ref[...])
            for part in range(8):
                index, row = piece_place(quarter, half * 8 + part)
                value = piece[part] if first_pass else values[part * HALF : (part + 1) * HALF]
                put_source(source, index, row, value * inverse[row : row + HALF, index : index + 1])

    @pl.when(first < count)
    def _():
        apply_loop(
            count, first, put_ref, take_ref, tiles_ref, source, total, False, tilde, inverse_ref
        )

    @pl.when(step == pl.num_programs(0) - 1)
    def _():
        rows = targets[0].shape[1]
        lines = lane_sums(tilde) if first_pass else None
        for number in range(16):
            if first_pass:
                line = lines[:, number * BLK : (number + 1) * BLK]
                total[number * rows + BLK : (number + 1) * rows, :BLK] = jnp.broadcast_to(
                    line, (rows - BLK, BLK)
                )
            targets[number // 8][number % 8] = total[number * rows : (number + 1) * rows, :]


def in_hbm(tiles):
    return pltpu.with_memory_space_constraint(tiles, pltpu.HBM)


def whole(shape):
    return pl.BlockSpec(shape, lambda s, *_: (0,) * len(shape), pipeline_mode=pl.Buffered(1))


def forward_call(count, put, take, tiles, inverse, factor, pieces):
    first_pass = factor is None
    slots = tiles.shape[0]
    width = pieces[0].shape[-1]
    rows = BLK + (8 if first_pass else 0)
    extra = [] if first_pass else [factor]
    out = jax.ShapeDtypeStruct((8, rows, width), F32)
    scratch = [pltpu.VMEM((32, 2 * BLK, width), BF16), pltpu.VMEM((16 * rows, width), F32)]
    if first_pass:
        scratch.append(pltpu.VMEM((16, BLK, BLK), F32))
    return pl.pallas_call(
        functools.partial(forward_kernel, first_pass),
        out_shape=(out,) * 2,
        grid_spec=pltpu.PrefetchScalarGridSpec(
            num_scalar_prefetch=3,
            grid=(slots // CHUNK,),
            in_specs=[pl.BlockSpec((CHUNK, BLK, BLK), chunk_map)]
            + [whole(a.shape) for a in [inverse] + extra + list(pieces)],
            out_specs=(whole(out.shape),) * 2,
            scratch_shapes=scratch,
        ),
        compiler_params=pltpu.CompilerParams(vmem_limit_bytes=26 * 2**20),
        cost_estimate=pl.CostEstimate(
            flops=6 * 2**30, bytes_accessed=2**24, transcendentals=0
        ),
    )(count, put, take, in_hbm(tiles), inverse, *extra, *pieces)


def backward_kernel(*refs):
    count_ref, put_ref, take_ref, tiles_ref = refs[:4]
    pieces, outs, (source, total) = refs[4:12], refs[12:20], refs[20:]
    step = pl.program_id(0)
    count = count_ref[0]
    first = step * CHUNK

    @pl.when(step == 0)
    def _():
        total[...] = jnp.zeros_like(total)
        for number, piece in enumerate(pieces):
            for part in range(2):
                put_source(source, number * 2 + part, 0, piece[part])

    @pl.when(first < count)
    def _():
        apply_loop(count, first, put_ref, take_ref, tiles_ref, source, total, True, None, None)

    @pl.when(step == pl.num_programs(0) - 1)
    def _():
        for number, out in enumerate(outs):
            for part in range(8):
                index, row = piece_place(number // 2, number % 2 * 8 + part)
                out[part] = total[index * BLK + row : index * BLK + row + HALF, :]


def backward_call(count, put, take, tiles, pieces):
    slots = tiles.shape[0]
    width = pieces[0].shape[-1]
    out = jax.ShapeDtypeStruct((8, HALF, width), F32)
    return pl.pallas_call(
        backward_kernel,
        out_shape=(out,) * 8,
        grid_spec=pltpu.PrefetchScalarGridSpec(
            num_scalar_prefetch=3,
            grid=(slots // CHUNK,),
            in_specs=[pl.BlockSpec((CHUNK, BLK, BLK), chunk_map)]
            + [whole(a.shape) for a in pieces],
            out_specs=(whole(out.shape),) * 8,
            scratch_shapes=[
                pltpu.VMEM((16, 2 * BLK, width), BF16),
                pltpu.VMEM((32 * BLK, width), F32),
            ],
        ),
        compiler_params=pltpu.CompilerParams(vmem_limit_bytes=26 * 2**20),
        cost_estimate=pl.CostEstimate(
            flops=6 * 2**30, bytes_accessed=2**24, transcendentals=0
        ),
    )(count, put, take, in_hbm(tiles), *pieces)


PANEL = 32


def inverse_factor_kernel(one_ref, two_ref, out_ref, work, columns, multiplier, right):
    size = out_ref.shape[0]
    lanes = columns.shape[-1]
    half, quarter = size // 2, size // 4
    work[:half, :half] = one_ref[:half]
    work[:quarter, half:size] = one_ref[half:]
    work[quarter:half, half:size] = two_ref[:quarter]
    work[half:, half:size] = two_ref[quarter:]
    work[half:, :half] = jnp.zeros((half, half), F32)
    row_at = lax.broadcasted_iota(jnp.int32, (size, size), 0)
    lane_at = lax.broadcasted_iota(jnp.int32, (size, size), 1)
    work[:, size:] = (row_at == lane_at).astype(F32)
    row_small = lax.broadcasted_iota(jnp.int32, (PANEL, lanes), 0)
    lane_small = lax.broadcasted_iota(jnp.int32, (PANEL, lanes), 1)
    unit = (row_small == lane_small).astype(F32)
    for start in range(0, size, PANEL):
        end = start + PANEL
        corner = work[start:end, start:end]
        for k in range(PANEL):
            columns[k] = jnp.broadcast_to(corner[:, k : k + 1], (PANEL, lanes))
        right[...] = unit
        for j in range(PANEL - 1):
            low = 8 * ((j + 1) // 8)
            column = columns[j, low:, :]
            factor = jnp.where(row_small[low:] > j, column, 0.0) * (1.0 / columns[j, j : j + 1, :])
            multiplier[low:, :] = factor
            for k in range(j + 1, PANEL):
                k_low = 8 * (k // 8)
                columns[k, k_low:, :] -= column[k_low - low :] * multiplier[k : k + 1, :]
            right[low:, :] -= factor * right[j : j + 1, :]
        pivots = jnp.concatenate([columns[k, k : k + 1, :] for k in range(PANEL)], axis=0)
        corner = (right[...] * (1.0 / jnp.sqrt(pivots)))[:, :PANEL]
        left = lanes * (start // lanes)
        used = size + lanes * ((end + lanes - 1) // lanes)
        panel = jnp.dot(
            corner, work[start:end, left:used], precision=HIGHEST, preferred_element_type=F32
        )
        work[start:end, left:used] = panel
        if end < size:
            update = lax.dot_general(
                panel[:, : size - left],
                panel,
                (((0,), (0,)), ((), ())),
                precision=HIGHEST,
                preferred_element_type=F32,
            )
            work[end:, left:used] -= update[end - left :, :]
    out_ref[...] = work[:, size:]


def inverse_factor(one, two):
    size = 2 * one.shape[1]
    return pl.pallas_call(
        inverse_factor_kernel,
        out_shape=jax.ShapeDtypeStruct((size, size), F32),
        in_specs=[pl.BlockSpec(memory_space=pltpu.VMEM)] * 2,
        out_specs=pl.BlockSpec(memory_space=pltpu.VMEM),
        scratch_shapes=[
            pltpu.VMEM((size, 2 * size), F32),
            pltpu.VMEM((PANEL, PANEL, BLK), F32),
            pltpu.VMEM((PANEL, BLK), F32),
            pltpu.VMEM((PANEL, BLK), F32),
        ],
        compiler_params=pltpu.CompilerParams(vmem_limit_bytes=12 * 2**20),
        cost_estimate=pl.CostEstimate(flops=2**34, bytes_accessed=2**19, transcendentals=0),
    )(one, two)


def gather_light(value):
    return [
        jnp.concatenate(gather(value[None, half * BLK : (half + 1) * BLK], LIGHT[half]))
        for half in range(2)
    ]


def gather_heavy(halves):
    pieces = []
    for number, steps in enumerate(HEAVY):
        row = number % 2 * HALF
        pieces += gather(halves[number // 2][:, row : row + HALF], steps)
    return pieces


def scatter_row(outs):
    parts = []
    for half in range(2):
        pair = [
            scatter(outs[2 * number], outs[2 * number + 1], HEAVY[number])
            for number in (2 * half, 2 * half + 1)
        ]
        pair = jnp.concatenate(pair, axis=1)
        parts.append(scatter(pair[:2], pair[2:], LIGHT[half])[0])
    return jnp.concatenate(parts, axis=0)


def scatter_col(keep, send):
    got = flip(send, CORE)
    parts = []
    for half, steps in enumerate(COL_STEPS):
        low, high = slice(4 * half, 4 * half + 2), slice(4 * half + 2, 4 * half + 4)
        parts.append(scatter(keep[low] + got[low], keep[high] + got[high], steps)[0])
    return parts


def gather_col(value):
    pieces = []
    for half, steps in enumerate(COL_STEPS):
        pieces += gather(value[None, half * BLK : (half + 1) * BLK], steps)
    return pieces + [flip(piece, CORE) for piece in pieces]


def gram_sum(gram):
    half = gram.shape[0] // 2
    core = lax.axis_index("c")
    halves = [
        jnp.concatenate([gram[:half, :half], gram[: half // 2, half:]]),
        jnp.concatenate([gram[half // 2 : half, half:], gram[half:, half:]]),
    ]
    value = jnp.where(core == 0, *halves) + flip(jnp.where(core == 0, *halves[::-1]), CORE)
    for step in (X1, X3, Y1, Y3, Z1, Z3):
        value = value + flip(value, step)
    other = flip(value, CORE)
    return jnp.where(core == 0, value, other), jnp.where(core == 0, other, value)


def local(trial_vectors, tiles, tile_rows, tile_cols, tile_count):
    x, y, z, core = [lax.axis_index(a) for a in ("x", "y", "z", "c")]
    slots = tiles.shape[2]
    width = trial_vectors.shape[1]
    tiles = tiles.reshape(slots, BLK, BLK)
    count = tile_count.reshape(1)

    row = tile_rows.reshape(slots)
    col = tile_cols.reshape(slots)
    near, far = flip_bits(z, row // 4)
    part = row % 2
    slab = ((row // 2) % 2 ^ core) * 8 + jnp.where(part == 0, near + 2 * far, 4 + far + 2 * near)
    near_x, far_x = flip_bits(x, col // 8)
    near_y, far_y = flip_bits(y, (col // 2) % 4)
    at_x, at_y = near_x + 2 * far_x, near_y + 2 * far_y
    member = jnp.where(col % 2 == 0, at_x + 4 * at_y, 16 + at_y + 4 * at_x)
    put_first = jnp.concatenate([slab * (BLK + 8), slab])
    put_later = slab * BLK
    put_backward = member * BLK

    begun = gather_light(trial_vectors)
    pieces = gather_heavy(begun)

    sums = rowsum_call(
        count, (slab // 8) * 8 + (near + 2 * far) * 2 + part, tiles, 16, begun
    ).reshape(2, 2, 2, 2, BLK)
    got = sums[0] + flip(sums[1], CORE)
    inverse_own = 1.0 / (1.0 + scatter(got[0], got[1], COL_STEPS[0])[0])
    gathered = jnp.concatenate(gather(inverse_own[None], LIGHT[0] + LIGHT[1]))
    inverse = jnp.concatenate(
        [gathered[:, 0], gathered[:, 1].reshape(4, 4, BLK).swapaxes(0, 1).reshape(16, BLK)]
    )
    inverse_own = inverse_own.reshape(2 * BLK, 1)

    vectors = trial_vectors
    factor = None
    scale = None
    for iteration in range(ITERS):
        outs = forward_call(
            count,
            put_first if iteration == 0 else put_later,
            member,
            tiles,
            inverse,
            factor,
            pieces,
        )
        one, two = scatter_col(*outs)
        if iteration == 0:
            tilde = jnp.concatenate([one[BLK, :BLK], two[BLK, :BLK]]).reshape(2 * BLK, 1)
            scale = inverse_own / (inverse_own * (inverse_own + tilde))
        summed = jnp.concatenate([one[:BLK], two[:BLK]])
        weighted = scale * (scale * (summed + inverse_own * vectors))
        outs = backward_call(count, put_backward, slab, tiles, gather_col(weighted))
        reduced = inverse_own * (scatter_row(outs) + weighted)
        gram = lax.dot_general(
            reduced,
            reduced,
            (((0,), (0,)), ((), ())),
            precision=HIGHEST,
            preferred_element_type=F32,
        )
        if iteration + 1 < ITERS:
            pieces = gather_heavy(gather_light(reduced))
        factor = inverse_factor(*gram_sum(gram))
        vectors = nt_dot(reduced, factor)
    total_nodes = 2 * BLK * 128
    return vectors * math.sqrt(total_nodes)


def solution(mesh):
    fine = Mesh(mesh.devices.reshape(4, 4, 4, 2), ("x", "y", "z", "c"))
    row, column = ("x", "y"), ("z", "c")
    in_specs = (
        P(row + column, None),
        P(row, column, None, None, None),
        P(row, column, None),
        P(row, column, None),
        P(row, column),
    )
    return jax.shard_map(
        local, mesh=fine, in_specs=in_specs, out_specs=P(row + column, None), check_vma=False
    )
```

```python
import functools
import math

import jax
import jax.numpy as jnp
from jax import lax
from jax.experimental import pallas as pl
from jax.experimental.pallas import tpu as pltpu
from jax.sharding import Mesh
from jax.sharding import PartitionSpec as P

ITERS = 2
HIGHEST = lax.Precision.HIGHEST
F32 = jnp.float32
BF16 = jnp.bfloat16
BLK = 128
HALF = 64
UNROLL = 16


def flip(value, step):
    axis, mask = step
    return lax.ppermute(value, axis, [(i, i ^ mask) for i in range(2 if axis == "c" else 4)])


def gather(value, steps):
    for step in steps[:-1]:
        value = jnp.concatenate([value, flip(value, step)])
    return [value, flip(value, steps[-1])]


def scatter(keep, send, steps):
    for step in reversed(steps[1:]):
        got = flip(send, step)
        half = keep.shape[0] // 2
        keep, send = keep[:half] + got[:half], keep[half:] + got[half:]
    return keep + flip(send, steps[0])


X1, X3, Y1, Y3, Z1, Z3 = [(axis, mask) for axis in "xyz" for mask in (1, 3)]
CORE = ("c", 1)
LIGHT = [[X1, X3], [Y1, Y3]]
HEAVY = [[Y1, Y3], [Y3, Y1], [X1, X3], [X3, X1]]
COL_STEPS = [[Z1, Z3], [Z3, Z1]]


def flip_bits(mine, other):
    offset = mine ^ other
    return jnp.where((offset == 1) | (offset == 2), 1, 0), jnp.where(offset >= 2, 1, 0)


def swapped(index):
    return (index & 3) + (index & 4) * 2 + (index & 8) // 2


def split(value):
    high = value.astype(BF16)
    return high, (value - high.astype(F32)).astype(BF16)


def nt_dot(a, b, precision=HIGHEST):
    return lax.dot_general(
        a, b, (((1,), (1,)), ((), ())), precision=precision, preferred_element_type=F32
    )


def lane_sums(total):
    lanes = total.shape[-1]
    return nt_dot(jnp.ones((8, lanes), F32), total[...].reshape(-1, lanes))[0:1, :]


def live_tile(tiles_ref, slot, first, count):
    return jnp.where(first + slot < count, tiles_ref[slot], 0.0)


def each_tile(count, one):
    def group(number, carry):
        for k in range(UNROLL):
            one(number * UNROLL + k, 0)
        return carry

    lax.fori_loop(0, (count + UNROLL - 1) // UNROLL, group, 0)


def rowsum_kernel(count_ref, put_ref, tiles_ref, *refs):
    out_ref, total = refs[-2:]
    step = pl.program_id(0)
    count = count_ref[0]

    @pl.when(step == 0)
    def _():
        total[...] = jnp.zeros_like(total)

    first = 0

    @pl.when(first < count)
    def _():
        def one(slot, carry):
            block = put_ref[first + slot]
            total[block] += live_tile(tiles_ref, slot, first, count)
            return carry

        each_tile(count, one)

    @pl.when(step == pl.num_programs(0) - 1)
    def _():
        out_ref[...] = lane_sums(total)


def rowsum_call(count, put, tiles, out_blocks, after):
    slots = tiles.shape[0]
    return pl.pallas_call(
        rowsum_kernel,
        out_shape=jax.ShapeDtypeStruct((1, out_blocks * BLK), F32),
        grid_spec=pltpu.PrefetchScalarGridSpec(
            num_scalar_prefetch=2,
            grid=(1,),
            in_specs=[whole(tiles.shape)]
            + [pl.BlockSpec(memory_space=pl.ANY)] * len(after),
            out_specs=pl.BlockSpec((1, out_blocks * BLK), lambda s, *_: (0, 0)),
            scratch_shapes=[pltpu.VMEM((out_blocks, BLK, BLK), F32)],
        ),
        compiler_params=pltpu.CompilerParams(vmem_limit_bytes=12 * 2**20),
        cost_estimate=pl.CostEstimate(flops=10**10, bytes_accessed=2**23, transcendentals=0),
    )(count, put, tiles, *after)


def apply_loop(
    count, first, put_ref, take_ref, tiles_ref, source, total, adjoint, tilde, inverse_ref
):
    def one(slot, carry):
        tile = live_tile(tiles_ref, slot, first, count)
        take = take_ref[first + slot]
        put = pl.multiple_of(put_ref[first + slot], 8)
        if tilde is not None:
            tilde_block = put_ref[put_ref.shape[0] // 2 + first + slot]
            tilde[tilde_block] += tile * inverse_ref[pl.ds(take, 1), :]
        if adjoint:
            tile = tile.T
        high, low = split(tile)
        product = jnp.dot(
            jnp.concatenate([high, high], axis=1), source[take], preferred_element_type=F32
        ) + jnp.dot(low, source[take, :BLK], preferred_element_type=F32)
        total[pl.ds(put, BLK), :] += product
        return carry

    each_tile(count, one)


def put_source(source, index, row, value):
    high, low = split(value)
    rows = value.shape[0]
    source[index, row : row + rows] = high
    source[index, BLK + row : BLK + row + rows] = low


def piece_place(quarter, index):
    place = index if quarter % 2 == 0 else swapped(index)
    return (quarter // 2) * 16 + place, (quarter % 2) * HALF


def forward_kernel(first_pass, *refs):
    count_ref, put_ref, take_ref, tiles_ref, inverse_ref = refs[:5]
    factor_ref = None
    refs = refs[5:]
    if not first_pass:
        factor_ref, refs = refs[0], refs[1:]
    pieces, targets, refs = refs[:8], refs[8:10], refs[10:]
    source, total = refs[:2]
    tilde = refs[2] if first_pass else None
    step = pl.program_id(0)
    count = count_ref[0]
    first = 0

    @pl.when(step == 0)
    def _():
        total[...] = jnp.zeros_like(total)
        if first_pass:
            tilde[...] = jnp.zeros_like(tilde)
        inverse = inverse_ref[...].T
        for number, piece in enumerate(pieces):
            quarter, half = number // 2, number % 2
            if not first_pass:
                values = nt_dot(piece[...].reshape(8 * HALF, -1), factor_ref[...])
            for part in range(8):
                index, row = piece_place(quarter, half * 8 + part)
                value = piece[part] if first_pass else values[part * HALF : (part + 1) * HALF]
                put_source(source, index, row, value * inverse[row : row + HALF, index : index + 1])

    @pl.when(first < count)
    def _():
        apply_loop(
            count, first, put_ref, take_ref, tiles_ref, source, total, False, tilde, inverse_ref
        )

    @pl.when(step == pl.num_programs(0) - 1)
    def _():
        rows = targets[0].shape[1]
        lines = lane_sums(tilde) if first_pass else None
        for number in range(16):
            if first_pass:
                line = lines[:, number * BLK : (number + 1) * BLK]
                total[number * rows + BLK : (number + 1) * rows, :BLK] = jnp.broadcast_to(
                    line, (rows - BLK, BLK)
                )
            targets[number // 8][number % 8] = total[number * rows : (number + 1) * rows, :]


def whole(shape):
    return pl.BlockSpec(shape, lambda s, *_: (0,) * len(shape), pipeline_mode=pl.Buffered(1))


def forward_call(count, put, take, tiles, inverse, factor, pieces):
    first_pass = factor is None
    slots = tiles.shape[0]
    width = pieces[0].shape[-1]
    rows = BLK + (8 if first_pass else 0)
    extra = [] if first_pass else [factor]
    out = jax.ShapeDtypeStruct((8, rows, width), F32)
    scratch = [pltpu.VMEM((32, 2 * BLK, width), BF16), pltpu.VMEM((16 * rows, width), F32)]
    if first_pass:
        scratch.append(pltpu.VMEM((16, BLK, BLK), F32))
    return pl.pallas_call(
        functools.partial(forward_kernel, first_pass),
        out_shape=(out,) * 2,
        grid_spec=pltpu.PrefetchScalarGridSpec(
            num_scalar_prefetch=3,
            grid=(1,),
            in_specs=[whole(tiles.shape)]
            + [whole(a.shape) for a in [inverse] + extra + list(pieces)],
            out_specs=(whole(out.shape),) * 2,
            scratch_shapes=scratch,
        ),
        compiler_params=pltpu.CompilerParams(vmem_limit_bytes=26 * 2**20),
        cost_estimate=pl.CostEstimate(
            flops=6 * 2**30, bytes_accessed=2**24, transcendentals=0
        ),
    )(count, put, take, tiles, inverse, *extra, *pieces)


def backward_kernel(*refs):
    count_ref, put_ref, take_ref, tiles_ref = refs[:4]
    pieces, outs, (source, total) = refs[4:12], refs[12:20], refs[20:]
    step = pl.program_id(0)
    count = count_ref[0]
    first = 0

    @pl.when(step == 0)
    def _():
        total[...] = jnp.zeros_like(total)
        for number, piece in enumerate(pieces):
            for part in range(2):
                put_source(source, number * 2 + part, 0, piece[part])

    @pl.when(first < count)
    def _():
        apply_loop(count, first, put_ref, take_ref, tiles_ref, source, total, True, None, None)

    @pl.when(step == pl.num_programs(0) - 1)
    def _():
        for number, out in enumerate(outs):
            for part in range(8):
                index, row = piece_place(number // 2, number % 2 * 8 + part)
                out[part] = total[index * BLK + row : index * BLK + row + HALF, :]


def backward_call(count, put, take, tiles, pieces):
    slots = tiles.shape[0]
    width = pieces[0].shape[-1]
    out = jax.ShapeDtypeStruct((8, HALF, width), F32)
    return pl.pallas_call(
        backward_kernel,
        out_shape=(out,) * 8,
        grid_spec=pltpu.PrefetchScalarGridSpec(
            num_scalar_prefetch=3,
            grid=(1,),
            in_specs=[whole(tiles.shape)]
            + [whole(a.shape) for a in pieces],
            out_specs=(whole(out.shape),) * 8,
            scratch_shapes=[
                pltpu.VMEM((16, 2 * BLK, width), BF16),
                pltpu.VMEM((32 * BLK, width), F32),
            ],
        ),
        compiler_params=pltpu.CompilerParams(vmem_limit_bytes=26 * 2**20),
        cost_estimate=pl.CostEstimate(
            flops=6 * 2**30, bytes_accessed=2**24, transcendentals=0
        ),
    )(count, put, take, tiles, *pieces)


PANEL = 32


def inverse_factor_kernel(one_ref, two_ref, out_ref, work, columns, multiplier, right):
    size = out_ref.shape[0]
    lanes = columns.shape[-1]
    half, quarter = size // 2, size // 4
    work[:half, :half] = one_ref[:half]
    work[:quarter, half:size] = one_ref[half:]
    work[quarter:half, half:size] = two_ref[:quarter]
    work[half:, half:size] = two_ref[quarter:]
    work[half:, :half] = jnp.zeros((half, half), F32)
    row_at = lax.broadcasted_iota(jnp.int32, (size, size), 0)
    lane_at = lax.broadcasted_iota(jnp.int32, (size, size), 1)
    work[:, size:] = (row_at == lane_at).astype(F32)
    row_small = lax.broadcasted_iota(jnp.int32, (PANEL, lanes), 0)
    lane_small = lax.broadcasted_iota(jnp.int32, (PANEL, lanes), 1)
    unit = (row_small == lane_small).astype(F32)
    for start in range(0, size, PANEL):
        end = start + PANEL
        corner = work[start:end, start:end]
        for k in range(PANEL):
            columns[k] = jnp.broadcast_to(corner[:, k : k + 1], (PANEL, lanes))
        right[...] = unit
        for j in range(PANEL - 1):
            low = 8 * ((j + 1) // 8)
            column = columns[j, low:, :]
            factor = jnp.where(row_small[low:] > j, column, 0.0) * (1.0 / columns[j, j : j + 1, :])
            multiplier[low:, :] = factor
            for k in range(j + 1, PANEL):
                k_low = 8 * (k // 8)
                columns[k, k_low:, :] -= column[k_low - low :] * multiplier[k : k + 1, :]
            right[low:, :] -= factor * right[j : j + 1, :]
        pivots = jnp.concatenate([columns[k, k : k + 1, :] for k in range(PANEL)], axis=0)
        corner = (right[...] * (1.0 / jnp.sqrt(pivots)))[:, :PANEL]
        left = lanes * (start // lanes)
        used = size + lanes * ((end + lanes - 1) // lanes)
        panel = jnp.dot(
            corner, work[start:end, left:used], precision=HIGHEST, preferred_element_type=F32
        )
        work[start:end, left:used] = panel
        if end < size:
            update = lax.dot_general(
                panel[:, : size - left],
                panel,
                (((0,), (0,)), ((), ())),
                precision=HIGHEST,
                preferred_element_type=F32,
            )
            work[end:, left:used] -= update[end - left :, :]
    out_ref[...] = work[:, size:]


def inverse_factor(one, two):
    size = 2 * one.shape[1]
    return pl.pallas_call(
        inverse_factor_kernel,
        out_shape=jax.ShapeDtypeStruct((size, size), F32),
        in_specs=[pl.BlockSpec(memory_space=pltpu.VMEM)] * 2,
        out_specs=pl.BlockSpec(memory_space=pltpu.VMEM),
        scratch_shapes=[
            pltpu.VMEM((size, 2 * size), F32),
            pltpu.VMEM((PANEL, PANEL, BLK), F32),
            pltpu.VMEM((PANEL, BLK), F32),
            pltpu.VMEM((PANEL, BLK), F32),
        ],
        compiler_params=pltpu.CompilerParams(vmem_limit_bytes=12 * 2**20),
        cost_estimate=pl.CostEstimate(flops=2**34, bytes_accessed=2**19, transcendentals=0),
    )(one, two)


def gather_light(value):
    return [
        jnp.concatenate(gather(value[None, half * BLK : (half + 1) * BLK], LIGHT[half]))
        for half in range(2)
    ]


def gather_heavy(halves):
    pieces = []
    for number, steps in enumerate(HEAVY):
        row = number % 2 * HALF
        pieces += gather(halves[number // 2][:, row : row + HALF], steps)
    return pieces


def scatter_row(outs):
    parts = []
    for half in range(2):
        pair = [
            scatter(outs[2 * number], outs[2 * number + 1], HEAVY[number])
            for number in (2 * half, 2 * half + 1)
        ]
        pair = jnp.concatenate(pair, axis=1)
        parts.append(scatter(pair[:2], pair[2:], LIGHT[half])[0])
    return jnp.concatenate(parts, axis=0)


def scatter_col(keep, send):
    got = flip(send, CORE)
    parts = []
    for half, steps in enumerate(COL_STEPS):
        low, high = slice(4 * half, 4 * half + 2), slice(4 * half + 2, 4 * half + 4)
        parts.append(scatter(keep[low] + got[low], keep[high] + got[high], steps)[0])
    return parts


def gather_col(value):
    pieces = []
    for half, steps in enumerate(COL_STEPS):
        pieces += gather(value[None, half * BLK : (half + 1) * BLK], steps)
    return pieces + [flip(piece, CORE) for piece in pieces]


def gram_sum(gram):
    half = gram.shape[0] // 2
    core = lax.axis_index("c")
    halves = [
        jnp.concatenate([gram[:half, :half], gram[: half // 2, half:]]),
        jnp.concatenate([gram[half // 2 : half, half:], gram[half:, half:]]),
    ]
    value = jnp.where(core == 0, *halves) + flip(jnp.where(core == 0, *halves[::-1]), CORE)
    for step in (X1, X3, Y1, Y3, Z1, Z3):
        value = value + flip(value, step)
    other = flip(value, CORE)
    return jnp.where(core == 0, value, other), jnp.where(core == 0, other, value)


def local(trial_vectors, tiles, tile_rows, tile_cols, tile_count):
    x, y, z, core = [lax.axis_index(a) for a in ("x", "y", "z", "c")]
    slots = tiles.shape[2]
    width = trial_vectors.shape[1]
    tiles = tiles.reshape(slots, BLK, BLK)
    count = tile_count.reshape(1)

    row = tile_rows.reshape(slots)
    col = tile_cols.reshape(slots)
    near, far = flip_bits(z, row // 4)
    part = row % 2
    slab = ((row // 2) % 2 ^ core) * 8 + jnp.where(part == 0, near + 2 * far, 4 + far + 2 * near)
    near_x, far_x = flip_bits(x, col // 8)
    near_y, far_y = flip_bits(y, (col // 2) % 4)
    at_x, at_y = near_x + 2 * far_x, near_y + 2 * far_y
    member = jnp.where(col % 2 == 0, at_x + 4 * at_y, 16 + at_y + 4 * at_x)
    put_first = jnp.concatenate([slab * (BLK + 8), slab])
    put_later = slab * BLK
    put_backward = member * BLK

    begun = gather_light(trial_vectors)
    pieces = gather_heavy(begun)

    sums = rowsum_call(
        count, (slab // 8) * 8 + (near + 2 * far) * 2 + part, tiles, 16, begun
    ).reshape(2, 2, 2, 2, BLK)
    got = sums[0] + flip(sums[1], CORE)
    inverse_own = 1.0 / (1.0 + scatter(got[0], got[1], COL_STEPS[0])[0])
    gathered = jnp.concatenate(gather(inverse_own[None], LIGHT[0] + LIGHT[1]))
    inverse = jnp.concatenate(
        [gathered[:, 0], gathered[:, 1].reshape(4, 4, BLK).swapaxes(0, 1).reshape(16, BLK)]
    )
    inverse_own = inverse_own.reshape(2 * BLK, 1)

    vectors = trial_vectors
    factor = None
    scale = None
    for iteration in range(ITERS):
        outs = forward_call(
            count,
            put_first if iteration == 0 else put_later,
            member,
            tiles,
            inverse,
            factor,
            pieces,
        )
        one, two = scatter_col(*outs)
        if iteration == 0:
            tilde = jnp.concatenate([one[BLK, :BLK], two[BLK, :BLK]]).reshape(2 * BLK, 1)
            scale = inverse_own / (inverse_own * (inverse_own + tilde))
        summed = jnp.concatenate([one[:BLK], two[:BLK]])
        weighted = scale * (scale * (summed + inverse_own * vectors))
        outs = backward_call(count, put_backward, slab, tiles, gather_col(weighted))
        reduced = inverse_own * (scatter_row(outs) + weighted)
        gram = lax.dot_general(
            reduced,
            reduced,
            (((0,), (0,)), ((), ())),
            precision=HIGHEST,
            preferred_element_type=F32,
        )
        if iteration + 1 < ITERS:
            pieces = gather_heavy(gather_light(reduced))
        factor = inverse_factor(*gram_sum(gram))
        vectors = nt_dot(reduced, factor)
    total_nodes = 2 * BLK * 128
    return vectors * math.sqrt(total_nodes)


def solution(mesh):
    fine = Mesh(mesh.devices.reshape(4, 4, 4, 2), ("x", "y", "z", "c"))
    row, column = ("x", "y"), ("z", "c")
    in_specs = (
        P(row + column, None),
        P(row, column, None, None, None),
        P(row, column, None),
        P(row, column, None),
        P(row, column),
    )
    return jax.shard_map(
        local, mesh=fine, in_specs=in_specs, out_specs=P(row + column, None), check_vma=False
    )
```
